512 devices in a mesh: gx: 64 (over y, z), ta: 8 (over x, core).
Axes of the slice: x: 4, y: 4, z: 16, core: 2. Of those that a mesh axis runs over, the one named last changes fastest.
Arguments:
- query_vecs: bfloat16 [256, 64, 5120], P('gx', None, 'ta'), may hold values from -32 to 32
- key_vecs: bfloat16 [256, 64, 5120], P('gx', None, 'ta'), may hold values from -6 to 6
- value_vecs: bfloat16 [256, 64, 5120], P('gx', None, 'ta'), may hold values from -6 to 6
- slot_map: int32 [16, 64], replicated, may hold values from 0 to 63, each once within a row
- edge_list: int32 [256, 2], replicated, may hold values from 0 to 63
- edge_types: int32 [256], replicated, may hold values from 0 to 2
- type_gain: float32 [2, 3, 5120], P(None, None, 'ta'), may hold values from 0.25 to 2
- norm_gain: float32 [2, 5120], P(None, 'ta'), may hold values from 0.5 to 2
- gate_proj: bfloat16 [2, 5120, 20480], P(None, 'ta', 'gx'), may hold values from -0.078125 to 0.078125
- up_proj: bfloat16 [2, 5120, 20480], P(None, 'ta', 'gx'), may hold values from -0.078125 to 0.078125
- down_proj: bfloat16 [2, 20480, 5120], P(None, 'gx', 'ta'), may hold values from -0.0390625 to 0.0390625
Outputs:
- node_states: bfloat16 [512, 5120], P('gx', 'ta')
The draws below stay inside these ranges and needn't reach their ends.
All inputs are finite; a program needn't handle non-finite values.
Results may differ from the reference program's by a relative error of at most 0.04.
Values may be sent and summed in bfloat16 or wider, within the bound.
A program may use at most 64 MiB of HBM per device.

```python
import math
import jax
import jax.numpy as jnp
import numpy as np
from jax import lax

D = 5120
HEAD_DIM = 128
FF = 20480
VENUES = 16
STEPS = 16
NODE_STEPS = 8
ROUNDS = 2
ETYPES = 3
INST_DEV = 1
INST = 64
PAIRS = 256
EDGES = 256
N_GX = 64


def paired_draw(key):
    shape_full = (VENUES, STEPS, INST, D)
    key_one = jax.random.fold_in(key, 101)
    key_two = jax.random.fold_in(key, 202)
    keyset = jax.random.truncated_normal(key_one, -6.0, 6.0, shape_full, jnp.float32)
    queries = jax.random.truncated_normal(key_two, -6.0, 6.0, shape_full, jnp.float32)
    return (queries.reshape(VENUES * STEPS, INST, D), keyset.reshape(VENUES * STEPS, INST, D))


def draw_query_vecs(key, part):
    return paired_draw(key)[0].astype(jnp.bfloat16)


def draw_key_vecs(key, part):
    return paired_draw(key)[1].astype(jnp.bfloat16)


def plant(entries, stream_key, smallest, high):
    longest = entries.shape.index(max(entries.shape))
    spots = []
    for shift in (0, 1):
        where = [jax.random.randint(jax.random.fold_in(stream_key, axis), (), 0, length) for axis, length in enumerate(entries.shape)]
        where[longest] = (where[longest] + shift) % entries.shape[longest]
        spots.append(tuple(where))
    return entries.at[spots[0]].set(smallest).at[spots[1]].set(high)


def block_levels(own_key, extent, split, smallest, high):
    factor_of = 1.0
    for dim, blocks in split:
        steps = jax.random.uniform(jax.random.fold_in(jax.random.fold_in(own_key, 6), dim), (blocks,), jnp.float32, smallest / len(split), high / len(split))
        factor_of = factor_of * jnp.repeat(jnp.exp(steps), extent[dim] // blocks).reshape((-1,) + (1,) * (len(extent) - 1 - dim))
    return factor_of


def rank_table(number_of, lean):
    loads = [(1 << 20) // math.isqrt(rank ** lean) + 1 for rank in range(1, number_of + 1)]
    spread = 1 + sum(loads) // (1 << 30)
    return np.cumsum(np.array([max(1, weight // spread) for weight in loads]))


def skewed_ids(stream_key, dims, number_of, slope):
    listing = rank_table(number_of, slope)
    ticket = jax.random.randint(jax.random.fold_in(stream_key, 1), dims, 0, int(listing[number_of - 1]))
    standing = jnp.searchsorted(jnp.asarray(listing, jnp.int32), ticket, side="right")
    return jax.random.permutation(jax.random.fold_in(stream_key, 2), number_of)[standing].astype(jnp.int32)


def scatter_about(key, shape, deviation, most, split=(), held_as=jnp.bfloat16):
    values = deviation * jax.random.normal(key, shape, jnp.float32)
    if split:
        values = values * block_levels(key, shape, split, -0.22, 0.18)
    return jnp.clip(values, -most, most).astype(held_as)


def setup_inputs(seed: int = 0) -> dict:
    streams_of = jax.random.split(jax.random.key(seed), 12)
    return {
        "query_vecs": draw_query_vecs(jax.random.fold_in(streams_of[11], 71), 0),
        "key_vecs": draw_key_vecs(jax.random.fold_in(streams_of[11], 71), 0),
        "value_vecs": scatter_about(streams_of[2], (PAIRS, INST, D), 1.0, 6.0, ((0, 64), (2, 8))),
        "slot_map": jax.vmap(lambda own: jax.random.permutation(own, INST))(jax.random.split(streams_of[3], VENUES)).reshape((VENUES, INST)).astype(jnp.int32),
        "edge_list": plant(skewed_ids(streams_of[4], (EDGES, 2), INST, 2), jax.random.fold_in(streams_of[4], 3), 0, INST - 1).astype(jnp.int32),
        "edge_types": plant(jax.random.randint(streams_of[5], (EDGES,), 0, ETYPES), jax.random.fold_in(streams_of[5], 1), 0, ETYPES - 1).astype(jnp.int32),
        "type_gain": jnp.clip(jnp.exp(math.log(2.0) - 2.0794415 * jax.random.uniform(streams_of[6], (ROUNDS, ETYPES, D), jnp.float32) ** block_levels(streams_of[6], (ROUNDS, ETYPES, D), ((2, 8),), -0.2, 0.2)), 0.25, 2.0),
        "norm_gain": jnp.clip(jnp.exp(math.log(2.0) - 1.3862944 * jax.random.uniform(streams_of[7], (ROUNDS, D), jnp.float32) ** block_levels(streams_of[7], (ROUNDS, D), ((1, 8),), -0.2, 0.2)), 0.5, 2.0),
        "gate_proj": scatter_about(streams_of[8], (ROUNDS, D, FF), D ** -0.5, 0.078125, ((1, 8), (2, 64))),
        "up_proj": scatter_about(streams_of[9], (ROUNDS, D, FF), D ** -0.5, 0.078125, ((1, 8), (2, 64))),
        "down_proj": scatter_about(streams_of[10], (ROUNDS, FF, D), FF ** -0.5, 0.0390625, ((1, 64), (2, 8))),
    }


def reference(query_vecs, key_vecs, value_vecs, slot_map, edge_list, edge_types, type_gain, norm_gain, gate_proj, up_proj, down_proj):
    pair_total = VENUES * STEPS
    inst_total = INST_DEV * N_GX
    head_count = D // HEAD_DIM
    score_scale = 1.0 / HEAD_DIM ** 0.5
    pair_ids = jnp.arange(pair_total).astype(jnp.int32)
    venue_of = (pair_ids // STEPS).astype(jnp.int32)
    slot_order = slot_map[venue_of]
    query_steps = jnp.arange(VENUES * NODE_STEPS) % NODE_STEPS + (STEPS - NODE_STEPS)
    key_steps = jnp.arange(pair_total) % STEPS
    allowed = key_steps[None, :] <= query_steps[:, None]

    def attend_one(inst_idx):
        columns = slot_order[:, inst_idx].astype(jnp.int32)
        queries = query_vecs[pair_ids, columns]
        keyset = key_vecs[pair_ids, columns]
        valueset = value_vecs[pair_ids, columns]
        queries = queries.reshape(VENUES, STEPS, head_count, HEAD_DIM)[:, STEPS - NODE_STEPS:]
        queries = queries.reshape(VENUES * NODE_STEPS, head_count, HEAD_DIM)
        keyset = keyset.reshape(pair_total, head_count, HEAD_DIM)
        valueset = valueset.reshape(pair_total, head_count, HEAD_DIM)
        scores = jnp.einsum('qhd,khd->hqk', queries.astype(jnp.float32), keyset.astype(jnp.float32)) * score_scale
        scores = jnp.where(allowed[None], scores, jnp.float32(-1e+30))
        row_max = lax.optimization_barrier(jnp.max(scores, axis=-1, keepdims=True))
        expd = jnp.exp(scores - row_max)
        probs = (expd / lax.optimization_barrier(jnp.sum(expd, axis=-1, keepdims=True))).astype(jnp.bfloat16)
        attended = jnp.einsum('hqk,khd->qhd', probs.astype(jnp.float32), valueset.astype(jnp.float32))
        return lax.optimization_barrier(jnp.mean(attended.reshape(VENUES, NODE_STEPS, D), axis=0)).astype(jnp.bfloat16)
    nodes = lax.map(attend_one, jnp.arange(inst_total).astype(jnp.int32))
    nodes = nodes.reshape(inst_total * NODE_STEPS, D)
    node_ids = jnp.arange(inst_total).astype(jnp.int32)
    type_ids = jnp.arange(ETYPES).astype(jnp.int32)
    at_source = (edge_list[:, 0][:, None] == node_ids[None, :]).astype(jnp.float32)
    at_target = (edge_list[:, 1][:, None] == node_ids[None, :]).astype(jnp.float32)
    of_type = (edge_types[:, None] == type_ids[None, :]).astype(jnp.float32)
    adjacency = jnp.einsum('et,ei,ej->tij', of_type, at_target, at_source)
    degree = jnp.maximum(lax.optimization_barrier(jnp.sum(at_target, axis=0)), 1.0)
    adj_rows = adjacency.reshape(ETYPES * inst_total, inst_total).astype(jnp.bfloat16)
    for layer_idx in range(ROUNDS):
        flat_nodes = nodes.reshape(inst_total, NODE_STEPS * D)
        gathered = jnp.dot(adj_rows, flat_nodes, preferred_element_type=jnp.float32)
        gathered = gathered.reshape(ETYPES, inst_total, NODE_STEPS, D)
        message = lax.optimization_barrier(jnp.sum(gathered * type_gain[layer_idx][:, None, None, :], axis=0)) / degree[:, None, None]
        pre_norm = nodes.astype(jnp.float32) + message.reshape(inst_total * NODE_STEPS, D)
        row_scale = lax.rsqrt(lax.optimization_barrier(jnp.mean(pre_norm * pre_norm, axis=-1, keepdims=True)) + 1e-05)
        normed = (pre_norm * row_scale * norm_gain[layer_idx][None, :]).astype(jnp.bfloat16)
        gate_sum = jnp.dot(normed, gate_proj[layer_idx], preferred_element_type=jnp.float32)
        up_sum = jnp.dot(normed, up_proj[layer_idx], preferred_element_type=jnp.float32)
        hidden = (jax.nn.silu(gate_sum) * up_sum).astype(jnp.bfloat16)
        update = jnp.dot(hidden, down_proj[layer_idx], preferred_element_type=jnp.float32)
        nodes = (nodes.astype(jnp.float32) + update).astype(jnp.bfloat16)
    return nodes
```

```python
import functools

import jax
import jax.numpy as jnp
from jax import lax
from jax.experimental import pallas as pl
from jax.experimental.pallas import tpu as pltpu
from jax.sharding import PartitionSpec as P

MESH = pl.DeviceIdType.MESH
HEAD = 128
STEPS = 16
NSTEP = 8
ROUNDS = 2
ETYPES = 3
PD = 4
NZ = 16
NC = 2
F32 = jnp.float32
BF16 = jnp.bfloat16


def iota(shape, dim):
    return lax.broadcasted_iota(jnp.int32, shape, dim)


def kernel(
    gx,
    ta,
    q_hbm,
    k_hbm,
    v_hbm,
    slot_ref,
    edge_rows_ref,
    edge_cols_ref,
    tgain_ref,
    ngain_ref,
    g_hbm,
    u_hbm,
    d_hbm,
    out_ref,
    x_in,
    kv_send,
    kv_recv,
    q_send,
    q_recv,
    q_f32,
    gu_in,
    w_ref,
    d_ref,
    adj_ref,
    deg_ref,
    node_ref,
    part_ref,
    s_ref,
    yr_ref,
    zs_ref,
    zr_ref,
    gu_ref,
    cs_ref,
    cr_ref,
    xs_ref,
    xr_ref,
    sq_ref,
    sqr_ref,
    h_ref,
    in_sem,
    w_sem,
    kv_sems,
    q_sems,
    n_send,
    n_z,
    n_y,
    r_send,
    r_y,
    r_z,
    c_send,
    c_core,
    c_x,
    sq_sems,
    h_send,
    h_x,
    h_core,
):
    inst = gx
    nz = NZ if gx >= NZ else gx // 2
    ny = gx // nz
    nx = ta // NC
    feat = out_ref.shape[1]
    heads = feat // HEAD
    ffd = feat // 2
    rows = inst * NSTEP
    ch = rows // ta
    half = rows // 2
    me = lax.axis_index("gx")
    ti = lax.axis_index("ta")
    my_y, my_z = me // nz, me % nz
    my_x, my_c = ti // NC, ti % NC

    def gdev(y, z):
        return (y * nz + z, ti)

    barrier = pltpu.get_barrier_semaphore()

    def greet_gx(k, _):
        pl.semaphore_signal(
            barrier, inc=1, device_id=((me + k) % gx, ti), device_id_type=MESH
        )
        return 0

    lax.fori_loop(1, gx, greet_gx, 0)

    def greet_ta(k, _):
        pl.semaphore_signal(
            barrier, inc=1, device_id=(me, (ti + k) % ta), device_id_type=MESH
        )
        return 0

    lax.fori_loop(1, ta, greet_ta, 0)

    loads = [
        pltpu.make_async_copy(src, x_in.at[i], in_sem.at[i])
        for i, src in enumerate((q_hbm, k_hbm, v_hbm))
    ]
    loads[1].start()
    loads[2].start()
    loads[0].start()
    weights = [
        pltpu.make_async_copy(g_hbm, gu_in.at[0], w_sem.at[0]),
        pltpu.make_async_copy(u_hbm, gu_in.at[1], w_sem.at[1]),
        pltpu.make_async_copy(d_hbm, d_ref.at[:, pl.ds(0, ffd)], w_sem.at[2]),
    ]
    for w in weights:
        w.start()

    order = slot_ref[pl.ds(me * PD // STEPS, 1), :].astype(F32)
    r8 = iota((rows, inst), 0)
    pick = jnp.where(iota((rows, inst), 1) == r8 // NSTEP, order, 0.0)
    slot_of = jnp.sum(pick, axis=1, keepdims=True).astype(jnp.int32)
    row = iota((rows, 2 * PD * inst), 0)
    col = iota((rows, 2 * PD * inst), 1)
    perm = jnp.where(col == (row % NSTEP) * inst + slot_of, 1.0, 0.0).astype(BF16)

    loads[1].wait()
    loads[2].wait()
    keyvals = x_in[1:3].reshape(2 * PD * inst, feat)
    kv_send[...] = (
        jnp.dot(perm, keyvals, preferred_element_type=F32)
        .reshape(inst, NSTEP, feat)
        .astype(BF16)
    )
    loads[0].wait()
    queries = x_in[0].reshape(PD * inst, feat)
    q_send[...] = (
        jnp.dot(perm[:, : PD * inst], queries, preferred_element_type=F32)
        .reshape(inst, NSTEP, feat)[:, :PD]
        .astype(BF16)
    )
    pl.semaphore_wait(barrier, gx - 1 + ta - 1)

    def q_slot(g):
        return (g // 4) * 2 + g % 4 - 2

    has_q = me % 4 >= 2

    @pl.when(has_q)
    def _():
        def send_q(k, _):
            dest = (me + k) % gx
            pltpu.make_async_remote_copy(
                src_ref=q_send.at[dest],
                dst_ref=q_recv.at[q_slot(me)],
                send_sem=q_sems.at[0],
                recv_sem=q_sems.at[1],
                device_id=(dest, ti),
                device_id_type=MESH,
            ).start()
            return 0

        lax.fori_loop(1, gx, send_q, 0)
        pltpu.make_async_copy(
            q_send.at[me], q_recv.at[q_slot(me)], q_sems.at[1]
        ).start()

    def send_kv(k, _):
        dest = (me + k) % gx
        pltpu.make_async_remote_copy(
            src_ref=kv_send.at[dest],
            dst_ref=kv_recv.at[me],
            send_sem=kv_sems.at[0],
            recv_sem=kv_sems.at[1],
            device_id=(dest, ti),
            device_id_type=MESH,
        ).start()
        return 0

    lax.fori_loop(1, gx, send_kv, 0)
    pltpu.make_async_copy(kv_send.at[me], kv_recv.at[me], kv_sems.at[1]).start()

    tgt = edge_rows_ref[1:2, :]
    typ = edge_rows_ref[2:3, :]
    src = edge_cols_ref[:, 0:1]
    edges = tgt.shape[1]
    at_target = iota((rows, edges), 0) // NSTEP == tgt
    at_source = jnp.where(src == iota((edges, rows), 1) // NSTEP, 1.0, 0.0).astype(BF16)
    same_step = iota((rows, rows), 0) % NSTEP == iota((rows, rows), 1) % NSTEP
    for t in range(ETYPES):
        hit = jnp.where(at_target & (typ == t), 1.0, 0.0).astype(BF16)
        count = jnp.dot(hit, at_source, preferred_element_type=F32)
        adj_ref[t] = jnp.where(same_step, count, 0.0).astype(BF16)
    degree = jnp.sum(jnp.where(at_target, 1.0, 0.0), axis=1, keepdims=True)
    deg_ref[...] = jnp.broadcast_to(jnp.maximum(degree, 1.0), deg_ref.shape)

    for w in weights:
        w.wait()
    left = jnp.where(iota((ffd, feat), 0) == iota((ffd, feat), 1), 1.0, 0.0).astype(BF16)
    right = jnp.where(iota((ffd, feat), 0) + ffd == iota((ffd, feat), 1), 1.0, 0.0)
    right = right.astype(BF16)

    def place(r, _):
        w_ref[r] = (
            jnp.dot(gu_in[0, r], left, preferred_element_type=F32)
            + jnp.dot(gu_in[1, r], right, preferred_element_type=F32)
        ).astype(BF16)
        if d_ref.shape[1] > ffd:
            d_ref[r, ffd:, :] = jnp.zeros((d_ref.shape[1] - ffd, feat), BF16)
        return 0

    lax.fori_loop(0, ROUNDS, place, 0)

    pltpu.make_async_copy(q_recv, q_recv, q_sems.at[1]).wait()
    for j in range(q_recv.shape[0]):
        q_f32[j * PD : (j + 1) * PD, :] = q_recv[j].astype(F32)
    q_all = q_f32[...].astype(BF16)
    pltpu.make_async_copy(kv_recv, kv_recv, kv_sems.at[1]).wait()
    kv_all = kv_recv[...].astype(F32).reshape(rows, feat).astype(BF16)
    nq = q_all.shape[0]
    lane = iota((nq, rows), 1)
    key_step = (lane // NSTEP) % 4 * PD + lane % NSTEP
    q_step = iota((nq, rows), 0) % NSTEP + (STEPS - NSTEP)
    allowed = (lane % NSTEP < PD) & (key_step <= q_step)
    pooled = []
    for h in range(heads):
        cut = slice(h * HEAD, (h + 1) * HEAD)
        scores = lax.dot_general(
            q_all[:, cut],
            kv_all[:, cut],
            (((1,), (1,)), ((), ())),
            preferred_element_type=F32,
        ) * (1.0 / HEAD**0.5)
        scores = jnp.where(allowed, scores, -1e30)
        expd = jnp.exp(scores - jnp.max(scores, axis=1, keepdims=True))
        probs = expd / jnp.sum(expd, axis=1, keepdims=True)
        probs = pltpu.roll(probs, PD, 1).astype(BF16)
        att = jnp.dot(probs, kv_all[:, cut], preferred_element_type=F32)
        pooled.append(jnp.mean(att.reshape(nq // NSTEP, NSTEP, HEAD), axis=0))
    node_ref[0, me] = jnp.concatenate(pooled, axis=1).astype(BF16)

    eye = iota((rows, ch), 0) % ch == iota((rows, ch), 1)

    def one_round(r, _):
        nodes = node_ref.at[r]

        def send_z(j, _):
            k = jnp.where(j % 2 == 1, nz // 2 - j // 2, nz // 2 + j // 2)
            pltpu.make_async_remote_copy(
                src_ref=nodes.at[me],
                dst_ref=nodes.at[me],
                send_sem=n_send.at[r],
                recv_sem=n_z.at[r, k],
                device_id=gdev(my_y, (my_z + k) % nz),
                device_id_type=MESH,
            ).start()
            return 0

        lax.fori_loop(1, nz, send_z, 0)

        def pass_on(blk):
            for dy in range(1, ny):
                pltpu.make_async_remote_copy(
                    src_ref=nodes.at[blk],
                    dst_ref=nodes.at[blk],
                    send_sem=n_send.at[r],
                    recv_sem=n_y.at[r],
                    device_id=gdev((my_y + dy) % ny, my_z),
                    device_id_type=MESH,
                ).start()

        pass_on(me)

        def forward(j, _):
            k = jnp.where(j % 2 == 1, (j + 1) // 2, nz - j // 2)
            blk = my_y * nz + (my_z + nz - k) % nz
            pltpu.make_async_copy(nodes.at[blk], nodes.at[blk], n_z.at[r, k]).wait()
            pass_on(blk)
            return 0

        lax.fori_loop(1, nz, forward, 0)
        arrived = nodes.at[pl.ds(0, (ny - 1) * nz)]
        pltpu.make_async_copy(arrived, arrived, n_y.at[r]).wait()

        node_f32 = nodes[...].astype(F32).reshape(rows, feat)
        node_all = node_f32.astype(BF16)
        tgain = tgain_ref[r]
        squares = []
        for m in range(2):
            mine = slice(m * half, (m + 1) * half)
            total = jnp.zeros((half, feat), F32)
            for t in range(ETYPES):
                total += tgain[t : t + 1] * jnp.dot(
                    adj_ref[t, mine, :], node_all, preferred_element_type=F32
                )
            pre = node_f32[mine] + total / deg_ref[mine, 0:1]
            squares.append(jnp.sum(pre * pre, axis=1, keepdims=True))
            scaled = (pre * ngain_ref[pl.ds(r, 1), :]).astype(BF16)
            gu_ref[pl.ds(m * (ta // 2), ta // 2)] = jnp.dot(
                scaled, w_ref[r], preferred_element_type=F32
            ).reshape(ta // 2, ch, feat)
        square = jnp.concatenate(squares, axis=0)
        by_chunk = jnp.sum(jnp.where(eye, square, 0.0).reshape(ta, ch, ch), axis=1)
        sq_ref[r, :, 0:ch] = by_chunk

        def send_sq(k, _):
            pltpu.make_async_remote_copy(
                src_ref=sq_ref.at[r],
                dst_ref=sqr_ref.at[r, k],
                send_sem=sq_sems.at[r, 0],
                recv_sem=sq_sems.at[r, 1],
                device_id=(me, (ti + k) % ta),
                device_id_type=MESH,
            ).start()
            return 0

        for i in range(nx):
            x = (my_x + i + nx // 2) % nx
            cs_ref[r, i] = gu_ref[x * NC + 1 - my_c].astype(BF16)
            pltpu.make_async_remote_copy(
                src_ref=cs_ref.at[r, i],
                dst_ref=cr_ref.at[r, i],
                send_sem=c_send.at[r],
                recv_sem=c_core.at[r, i],
                device_id=(me, my_x * NC + 1 - my_c),
                device_id_type=MESH,
            ).start()
        lax.fori_loop(1, ta, send_sq, 0)
        total = jnp.zeros((ch, feat), F32)
        for i in range(nx):
            dx = (i + nx // 2) % nx
            x = (my_x + dx) % nx
            landed = cr_ref.at[r, i]
            pltpu.make_async_copy(landed, landed, c_core.at[r, i]).wait()
            chip_sum = gu_ref[x * NC + my_c] + cr_ref[r, i].astype(F32)
            if dx == 0:
                total = chip_sum
            else:
                xs_ref[r, dx - 1] = chip_sum.astype(BF16)
                pltpu.make_async_remote_copy(
                    src_ref=xs_ref.at[r, dx - 1],
                    dst_ref=xr_ref.at[r, dx - 1],
                    send_sem=c_send.at[r],
                    recv_sem=c_x.at[r],
                    device_id=(me, x * NC + my_c),
                    device_id_type=MESH,
                ).start()
        others = sqr_ref.at[r, pl.ds(1, ta - 1)]
        pltpu.make_async_copy(others, others, sq_sems.at[r, 1]).wait()
        sq_row = sq_ref[r, pl.ds(ti, 1), 0:ch]
        for k in range(1, ta):
            sq_row += sqr_ref[r, k, pl.ds(ti, 1), 0:ch]
        sq_col = jnp.sum(jnp.where(eye[:ch], sq_row, 0.0), axis=1, keepdims=True)
        row_scale = lax.rsqrt(sq_col / (feat * ta) + 1e-5)
        pltpu.make_async_copy(xr_ref.at[r], xr_ref.at[r], c_x.at[r]).wait()
        for i in range(nx - 1):
            total += xr_ref[r, i].astype(F32)
        total = total * row_scale
        acted = jax.nn.silu(total) * pltpu.roll(total, feat - ffd, 1)
        fpad = h_ref.shape[3]
        acted = jnp.where(iota((ch, fpad), 1) < ffd, acted[:, :fpad], 0.0)
        h_ref[r, ti] = acted.astype(BF16)

        for dx in (nx // 2, *[d for d in range(1, nx) if d != nx // 2]):
            pltpu.make_async_remote_copy(
                src_ref=h_ref.at[r, ti],
                dst_ref=h_ref.at[r, ti],
                send_sem=h_send.at[r],
                recv_sem=h_x.at[r, dx],
                device_id=(me, (my_x + dx) % nx * NC + my_c),
                device_id_type=MESH,
            ).start()
        for dx in (0, *[d for d in range(1, nx) if d != nx // 2], nx // 2):
            mine = (my_x + nx - dx) % nx * NC + my_c
            block = h_ref.at[r, mine]
            if dx:
                pltpu.make_async_copy(block, block, h_x.at[r, dx]).wait()
            pltpu.make_async_remote_copy(
                src_ref=block,
                dst_ref=block,
                send_sem=h_send.at[r],
                recv_sem=h_core.at[r],
                device_id=(me, my_x * NC + 1 - my_c),
                device_id_type=MESH,
            ).start()
        landed = h_ref.at[r, pl.ds(0, nx)]
        pltpu.make_async_copy(landed, landed, h_core.at[r]).wait()

        for m in range(2):
            hid = h_ref[r, pl.ds(m * (ta // 2), ta // 2)].reshape(half, fpad)
            down = jnp.dot(hid, d_ref[r], preferred_element_type=F32)
            down = down.reshape(inst // 2, NSTEP, feat)
            part_ref[pl.ds(m * (inst // 2), inst // 2)] = down
            s_ref[r, pl.ds(m * (inst // 2), inst // 2)] = down.astype(BF16)

        def send_y(j, _):
            k = jnp.where(j % 2 == 1, nz // 2 - j // 2, nz // 2 + j // 2)
            k = jnp.where(j == nz, 0, k)
            z = (my_z + k) % nz
            for dy in range(1, ny):
                y = (my_y + dy) % ny
                pltpu.make_async_remote_copy(
                    src_ref=s_ref.at[r, y * nz + z],
                    dst_ref=yr_ref.at[r, k, dy - 1],
                    send_sem=r_send.at[r],
                    recv_sem=r_y.at[r, k],
                    device_id=gdev(y, my_z),
                    device_id_type=MESH,
                ).start()
            return 0

        lax.fori_loop(1, nz + 1, send_y, 0)

        def column_sum(k):
            landed = yr_ref.at[r, k]
            pltpu.make_async_copy(landed, landed, r_y.at[r, k]).wait()
            acc = part_ref[my_y * nz + (my_z + k) % nz]
            for dy in range(ny - 1):
                acc += yr_ref[r, k, dy].astype(F32)
            return acc

        def reduce_y(j, _):
            k = jnp.where(j % 2 == 1, nz // 2 - j // 2, nz // 2 + j // 2)
            zs_ref[r, k] = column_sum(k).astype(BF16)
            pltpu.make_async_remote_copy(
                src_ref=zs_ref.at[r, k],
                dst_ref=zr_ref.at[r, k],
                send_sem=r_send.at[r],
                recv_sem=r_z.at[r],
                device_id=gdev(my_y, (my_z + k) % nz),
                device_id_type=MESH,
            ).start()
            return 0

        lax.fori_loop(1, nz, reduce_y, 0)
        acc = column_sum(0)
        landed = zr_ref.at[r, pl.ds(1, nz - 1)]
        pltpu.make_async_copy(landed, landed, r_z.at[r]).wait()
        for k in range(1, nz):
            acc += zr_ref[r, k].astype(F32)
        node_ref[r + 1, me] = (node_ref[r, me].astype(F32) + acc).astype(BF16)
        return 0

    lax.fori_loop(0, ROUNDS, one_round, 0)
    out_ref[...] = node_ref[ROUNDS, me]

    sent = kv_send.at[pl.ds(0, gx - 1)]
    pltpu.make_async_copy(sent, sent, kv_sems.at[0]).wait()

    @pl.when(has_q)
    def _():
        gone = q_send.at[pl.ds(0, gx - 1)]
        pltpu.make_async_copy(gone, gone, q_sems.at[0]).wait()

    def drain(r, _):
        n_out = nz - 1 + nz * (ny - 1)
        blocks = node_ref.at[0, pl.ds(0, n_out)]
        pltpu.make_async_copy(blocks, blocks, n_send.at[r]).wait()
        pltpu.make_async_copy(blocks, blocks, r_send.at[r]).wait()
        pltpu.make_async_copy(cs_ref.at[r], cs_ref.at[r], c_send.at[r]).wait()
        pltpu.make_async_copy(xs_ref.at[r], xs_ref.at[r], c_send.at[r]).wait()
        others = sqr_ref.at[r, pl.ds(1, ta - 1)]
        pltpu.make_async_copy(others, others, sq_sems.at[r, 0]).wait()
        hid = h_ref.at[r, pl.ds(0, 2 * nx - 1)]
        pltpu.make_async_copy(hid, hid, h_send.at[r]).wait()
        return 0

    lax.fori_loop(0, ROUNDS, drain, 0)


def per_device(
    query_vecs,
    key_vecs,
    value_vecs,
    slot_map,
    edge_list,
    edge_types,
    type_gain,
    norm_gain,
    gate_proj,
    up_proj,
    down_proj,
):
    gx, ta = lax.axis_size("gx"), lax.axis_size("ta")
    pairs, inst, feat = query_vecs.shape
    ffd = gate_proj.shape[2]
    fpad = pl.cdiv(ffd, 128) * 128
    rows = inst * NSTEP
    nz = NZ if gx >= NZ else gx // 2
    ny = gx // nz
    nx = ta // NC
    ch = rows // ta
    edge_rows = jnp.concatenate([edge_list.T, edge_types[None]], axis=0)
    vmem = pl.BlockSpec(memory_space=pltpu.VMEM)
    hbm = pl.BlockSpec(memory_space=pl.ANY)
    dma = pltpu.SemaphoreType.DMA
    R = ROUNDS
    return pl.pallas_call(
        functools.partial(kernel, gx, ta),
        out_shape=jax.ShapeDtypeStruct((NSTEP, feat), BF16),
        in_specs=[hbm, hbm, hbm, vmem, vmem, vmem, vmem, vmem, hbm, hbm, hbm],
        out_specs=vmem,
        scratch_shapes=[
            pltpu.VMEM((3, pairs, inst, feat), BF16),
            pltpu.VMEM((inst, NSTEP, feat), BF16),
            pltpu.VMEM((inst, NSTEP, feat), BF16),
            pltpu.VMEM((inst, pairs, feat), BF16),
            pltpu.VMEM((gx // 2, pairs, feat), BF16),
            pltpu.VMEM((gx // 2 * pairs, feat), F32),
            pltpu.VMEM((2, R, feat, ffd), BF16),
            pltpu.VMEM((R, feat, feat), BF16),
            pltpu.VMEM((R, fpad, feat), BF16),
            pltpu.VMEM((ETYPES, rows, rows), BF16),
            pltpu.VMEM((rows, 128), F32),
            pltpu.VMEM((R + 1, inst, NSTEP, feat), BF16),
            pltpu.VMEM((inst, NSTEP, feat), F32),
            pltpu.VMEM((R, inst, NSTEP, feat), BF16),
            pltpu.VMEM((R, nz, ny - 1, NSTEP, feat), BF16),
            pltpu.VMEM((R, nz, NSTEP, feat), BF16),
            pltpu.VMEM((R, nz, NSTEP, feat), BF16),
            pltpu.VMEM((ta, ch, feat), F32),
            pltpu.VMEM((R, nx, ch, feat), BF16),
            pltpu.VMEM((R, nx, ch, feat), BF16),
            pltpu.VMEM((R, nx - 1, ch, feat), BF16),
            pltpu.VMEM((R, nx - 1, ch, feat), BF16),
            pltpu.VMEM((R, ta, 128), F32),
            pltpu.VMEM((R, ta, ta, 128), F32),
            pltpu.VMEM((R, ta, ch, fpad), BF16),
            dma((3,)),
            dma((3,)),
            dma((2,)),
            dma((2,)),
            dma((R,)),
            dma((R, nz)),
            dma((R,)),
            dma((R,)),
            dma((R, nz)),
            dma((R,)),
            dma((R,)),
            dma((R, nx)),
            dma((R,)),
            dma((R, 2)),
            dma((R,)),
            dma((R, nx)),
            dma((R,)),
        ],
        compiler_params=pltpu.CompilerParams(
            collective_id=0, has_side_effects=True, vmem_limit_bytes=56 << 20
        ),
    )(
        query_vecs,
        key_vecs,
        value_vecs,
        slot_map,
        edge_rows,
        edge_list,
        type_gain,
        norm_gain,
        gate_proj,
        up_proj,
        down_proj,
    )


def solution(mesh):
    placed = (
        P("gx", None, "ta"),
        P("gx", None, "ta"),
        P("gx", None, "ta"),
        P(),
        P(),
        P(),
        P(None, None, "ta"),
        P(None, "ta"),
        P(None, "ta", "gx"),
        P(None, "ta", "gx"),
        P(None, "gx", "ta"),
    )
    return jax.shard_map(
        per_device, mesh=mesh, in_specs=placed, out_specs=P("gx", "ta"), check_vma=False
    )
```

```python
import functools

import jax
import jax.numpy as jnp
from jax import lax
from jax.experimental import pallas as pl
from jax.experimental.pallas import tpu as pltpu
from jax.sharding import PartitionSpec as P

MESH = pl.DeviceIdType.MESH
HEAD = 128
STEPS = 16
NSTEP = 8
ROUNDS = 2
ETYPES = 3
PD = 4
NZ = 16
NC = 2
F32 = jnp.float32
BF16 = jnp.bfloat16
NT = (((1,), (1,)), ((), ()))


def iota(shape, dim):
    return lax.broadcasted_iota(jnp.int32, shape, dim)


def kernel(
    gx,
    ta,
    q_hbm,
    k_hbm,
    v_hbm,
    slot_ref,
    edge_ref,
    type_ref,
    tgain_ref,
    ngain_ref,
    g_hbm,
    u_hbm,
    d_hbm,
    out_ref,
    x_in,
    kv_send,
    kv_recv,
    q_send,
    q_recv,
    q_f32,
    w_ref,
    d_ref,
    adj_ref,
    deg_ref,
    node_ref,
    part_ref,
    s_ref,
    yr_ref,
    zs_ref,
    zr_ref,
    gu_ref,
    cs_ref,
    cr_ref,
    xs_ref,
    xr_ref,
    sq_ref,
    sqr_ref,
    h_ref,
    square_ref,
    in_sem,
    w_sem,
    kv_sems,
    q_sems,
    kv_send_sem,
    q_send_sem,
    n_send,
    n_z,
    n_y,
    r_send,
    r_y,
    r_z,
    c_send,
    c_core,
    c_x,
    sq_sems,
    h_send,
    h_x,
    h_core,
):
    inst = gx
    nz = NZ if gx >= NZ else gx // 2
    ny = gx // nz
    nx = ta // NC
    feat = out_ref.shape[1]
    heads = feat // HEAD
    ffd = feat // 2
    rows = inst * NSTEP
    ch = rows // ta
    half = rows // 2
    c0 = (heads + 1) // 2 * HEAD
    cuts = (pl.ds(0, c0), pl.ds(c0, feat - c0))
    me = lax.axis_index("gx")
    ti = lax.axis_index("ta")
    my_y, my_z = me // nz, me % nz
    my_x, my_c = ti // NC, ti % NC

    def gdev(y, z):
        return (y * nz + z, ti)

    barrier = pltpu.get_barrier_semaphore()

    def greet_gx(k, _):
        pl.semaphore_signal(
            barrier, inc=1, device_id=((me + k) % gx, ti), device_id_type=MESH
        )
        return 0

    lax.fori_loop(1, gx, greet_gx, 0)

    def greet_ta(k, _):
        pl.semaphore_signal(
            barrier, inc=1, device_id=(me, (ti + k) % ta), device_id_type=MESH
        )
        return 0

    lax.fori_loop(1, ta, greet_ta, 0)

    loads = [
        pltpu.make_async_copy(src, x_in.at[i], in_sem.at[i])
        for i, src in enumerate((q_hbm, k_hbm, v_hbm))
    ]
    loads[1].start()
    loads[2].start()
    loads[0].start()
    weights = [
        pltpu.make_async_copy(g_hbm, w_ref.at[:, pl.ds(0, ffd)], w_sem.at[0]),
        pltpu.make_async_copy(u_hbm, w_ref.at[:, pl.ds(ffd, ffd)], w_sem.at[1]),
        pltpu.make_async_copy(d_hbm, d_ref.at[:, pl.ds(0, ffd)], w_sem.at[2]),
    ]

    order = slot_ref[pl.ds(me * PD // STEPS, 1), :].astype(F32)
    r8 = iota((rows, inst), 0)
    pick = jnp.where(iota((rows, inst), 1) == r8 // NSTEP, order, 0.0)
    slot_of = jnp.sum(pick, axis=1, keepdims=True).astype(jnp.int32)
    row = iota((rows, 2 * PD * inst), 0)
    col = iota((rows, 2 * PD * inst), 1)
    perm = jnp.where(col == (row % NSTEP) * inst + slot_of, 1.0, 0.0).astype(BF16)

    loads[1].wait()
    loads[2].wait()
    keyvals = x_in[1:3].reshape(2 * PD * inst, feat)
    kv_send[...] = (
        jnp.dot(perm, keyvals, preferred_element_type=F32)
        .reshape(inst, NSTEP, feat)
        .astype(BF16)
    )
    loads[0].wait()
    queries = x_in[0].reshape(PD * inst, feat)
    q_send[...] = (
        jnp.dot(perm[:, : PD * inst], queries, preferred_element_type=F32)
        .reshape(inst, NSTEP, feat)[:, :PD]
        .astype(BF16)
    )
    pl.semaphore_wait(barrier, gx - 1 + ta - 1)

    def q_slot(g):
        return (g // 4) * 2 + g % 4 - 2

    has_q = me % 4 >= 2

    for c, cut in enumerate(cuts):

        @pl.when(has_q)
        def _(c=c, cut=cut):
            def send_q(k, _):
                dest = (me + k) % gx
                pltpu.make_async_remote_copy(
                    src_ref=q_send.at[dest, :, cut],
                    dst_ref=q_recv.at[q_slot(me), :, cut],
                    send_sem=q_send_sem.at[0],
                    recv_sem=q_sems.at[c],
                    device_id=(dest, ti),
                    device_id_type=MESH,
                ).start()
                return 0

            lax.fori_loop(1, gx, send_q, 0)
            pltpu.make_async_copy(
                q_send.at[me, :, cut], q_recv.at[q_slot(me), :, cut], q_sems.at[c]
            ).start()

        def send_kv(k, _, c=c, cut=cut):
            dest = (me + k) % gx
            pltpu.make_async_remote_copy(
                src_ref=kv_send.at[dest, :, cut],
                dst_ref=kv_recv.at[me, :, cut],
                send_sem=kv_send_sem.at[0],
                recv_sem=kv_sems.at[c],
                device_id=(dest, ti),
                device_id_type=MESH,
            ).start()
            return 0

        lax.fori_loop(1, gx, send_kv, 0)
        pltpu.make_async_copy(
            kv_send.at[me, :, cut], kv_recv.at[me, :, cut], kv_sems.at[c]
        ).start()

    for w in weights:
        w.start()
    src = edge_ref[0:1, :]
    tgt = edge_ref[1:2, :]
    typ = type_ref[...]
    edges = tgt.shape[1]
    inst_of = iota((rows, edges), 0) // NSTEP
    at_target = inst_of == tgt
    at_source = jnp.where(inst_of == src, 1.0, 0.0).astype(BF16)
    same_step = iota((rows, rows), 0) % NSTEP == iota((rows, rows), 1) % NSTEP
    for t in range(ETYPES):
        hit = jnp.where(at_target & (typ == t), 1.0, 0.0).astype(BF16)
        count = lax.dot_general(hit, at_source, NT, preferred_element_type=F32)
        adj_ref[t] = jnp.where(same_step, count, 0.0).astype(BF16)
    degree = jnp.sum(jnp.where(at_target, 1.0, 0.0), axis=1, keepdims=True)
    deg_ref[...] = jnp.broadcast_to(jnp.maximum(degree, 1.0), deg_ref.shape)
    if d_ref.shape[1] > ffd:
        d_ref[:, ffd:, :] = jnp.zeros((ROUNDS, d_ref.shape[1] - ffd, feat), BF16)
    for w in weights:
        w.wait()

    nq = q_f32.shape[0]
    lane = iota((nq, rows), 1)
    key_step = (lane // NSTEP) % 4 * PD + lane % NSTEP
    q_step = iota((nq, rows), 0) % NSTEP + (STEPS - NSTEP)
    allowed = (lane % NSTEP < PD) & (key_step <= q_step)

    def attend(c, cut):
        whole = q_recv.at[:, :, cut]
        pltpu.make_async_copy(whole, whole, q_sems.at[c]).wait()
        for j in range(q_recv.shape[0]):
            q_f32[j * PD : (j + 1) * PD, cut] = q_recv[j, :, cut].astype(F32)
        q_all = q_f32[:, cut].astype(BF16)
        whole = kv_recv.at[:, :, cut]
        pltpu.make_async_copy(whole, whole, kv_sems.at[c]).wait()
        width = cut.size
        kv_all = kv_recv[:, :, cut].astype(F32).reshape(rows, width).astype(BF16)
        pooled = []
        for h in range(width // HEAD):
            own = slice(h * HEAD, (h + 1) * HEAD)
            scores = lax.dot_general(
                q_all[:, own], kv_all[:, own], NT, preferred_element_type=F32
            ) * (1.0 / HEAD**0.5)
            scores = jnp.where(allowed, scores, -1e30)
            expd = jnp.exp(scores - jnp.max(scores, axis=1, keepdims=True))
            probs = expd / jnp.sum(expd, axis=1, keepdims=True)
            probs = pltpu.roll(probs, PD, 1).astype(BF16)
            att = jnp.dot(probs, kv_all[:, own], preferred_element_type=F32)
            pooled.append(jnp.mean(att.reshape(nq // NSTEP, NSTEP, HEAD), axis=0))
        node_ref[0, me, :, cut] = jnp.concatenate(pooled, axis=1).astype(BF16)

    eye = iota((rows, ch), 0) % ch == iota((rows, ch), 1)

    if nz == 16:
        first = (8, 5, 11, 2, 14, 1, 15)
        second = {5: (2, 14, 1, 15), 11: (2, 14, 1, 15)}
        arrivals = (1, 15, 2, 14, 5, 11, 4, 6, 10, 12, 3, 7, 9, 13, 8)
    else:
        first = arrivals = tuple(range(1, nz))
        second = {}

    def pass_on(r, s, cut, blk):
        for dy in (2, 1, 3):
            if dy < ny:
                pltpu.make_async_remote_copy(
                    src_ref=node_ref.at[r, blk, :, cut],
                    dst_ref=node_ref.at[r, blk, :, cut],
                    send_sem=n_send.at[s],
                    recv_sem=n_y.at[s],
                    device_id=gdev((my_y + dy) % ny, my_z),
                    device_id_type=MESH,
                ).start()

    def send_z(r, s, cut, blk, step, total):
        pltpu.make_async_remote_copy(
            src_ref=node_ref.at[r, blk, :, cut],
            dst_ref=node_ref.at[r, blk, :, cut],
            send_sem=n_send.at[s],
            recv_sem=n_z.at[s, total],
            device_id=gdev(my_y, (my_z + step) % nz),
            device_id_type=MESH,
        ).start()

    def gather_start(r, s, cut):
        for k in first:
            send_z(r, s, cut, me, k, k)
        pass_on(r, s, cut, me)

    def gather_forward(r, s, cut):
        for k in arrivals:
            blk = my_y * nz + (my_z + nz - k) % nz
            landed = node_ref.at[r, blk, :, cut]
            pltpu.make_async_copy(landed, landed, n_z.at[s, k]).wait()
            for more in second.get(k, ()):
                send_z(r, s, cut, blk, more, (k + more) % nz)
            pass_on(r, s, cut, blk)

    def gather_end(r, s, cut):
        arrived = node_ref.at[r, pl.ds(0, (ny - 1) * nz), :, cut]
        pltpu.make_async_copy(arrived, arrived, n_y.at[s]).wait()

    def mix(r, c, cut):
        width = cut.size
        node_f32 = node_ref[r, :, :, cut].astype(F32).reshape(rows, width)
        node_all = node_f32.astype(BF16)
        ngain = ngain_ref[pl.ds(r, 1), cut]
        weight = w_ref[r, :, cut]
        for m in range(2):
            mine = slice(m * half, (m + 1) * half)
            total = jnp.zeros((half, width), F32)
            for t in range(ETYPES):
                total += tgain_ref[t, pl.ds(r, 1), cut] * jnp.dot(
                    adj_ref[t, mine, :], node_all, preferred_element_type=F32
                )
            pre = node_f32[mine] + total / deg_ref[mine, 0:1]
            square = jnp.sum(pre * pre, axis=1, keepdims=True)
            square = jnp.broadcast_to(square, (half, 128))
            scaled = (pre * ngain).astype(BF16)
            sums = lax.dot_general(scaled, weight, NT, preferred_element_type=F32)
            sums = sums.reshape(ta // 2, ch, feat)
            spot = slice(m * (ta // 2), (m + 1) * (ta // 2))
            if c == 0:
                gu_ref[spot] = sums
                square_ref[mine] = square
            else:
                gu_ref[spot] += sums
                square_ref[mine] += square

    def one_round(r, _):
        mix(r, 1, cuts[1])
        square = square_ref[:, 0:1]
        by_chunk = jnp.sum(jnp.where(eye, square, 0.0).reshape(ta, ch, ch), axis=1)
        sq_ref[r, :, 0:ch] = by_chunk

        def send_sq(k, _):
            pltpu.make_async_remote_copy(
                src_ref=sq_ref.at[r],
                dst_ref=sqr_ref.at[r, k],
                send_sem=sq_sems.at[r, 0],
                recv_sem=sq_sems.at[r, 1],
                device_id=(me, (ti + k) % ta),
                device_id_type=MESH,
            ).start()
            return 0

        for i in range(nx):
            x = (my_x + i + nx // 2) % nx
            cs_ref[r, i] = gu_ref[x * NC + 1 - my_c].astype(BF16)
            pltpu.make_async_remote_copy(
                src_ref=cs_ref.at[r, i],
                dst_ref=cr_ref.at[r, i],
                send_sem=c_send.at[r],
                recv_sem=c_core.at[r, i],
                device_id=(me, my_x * NC + 1 - my_c),
                device_id_type=MESH,
            ).start()
        lax.fori_loop(1, ta, send_sq, 0)
        total = jnp.zeros((ch, feat), F32)
        for i in range(nx):
            dx = (i + nx // 2) % nx
            x = (my_x + dx) % nx
            landed = cr_ref.at[r, i]
            pltpu.make_async_copy(landed, landed, c_core.at[r, i]).wait()
            chip_sum = gu_ref[x * NC + my_c] + cr_ref[r, i].astype(F32)
            if dx == 0:
                total = chip_sum
            else:
                xs_ref[r, dx - 1] = chip_sum.astype(BF16)
                pltpu.make_async_remote_copy(
                    src_ref=xs_ref.at[r, dx - 1],
                    dst_ref=xr_ref.at[r, dx - 1],
                    send_sem=c_send.at[r],
                    recv_sem=c_x.at[r],
                    device_id=(me, x * NC + my_c),
                    device_id_type=MESH,
                ).start()
        others = sqr_ref.at[r, pl.ds(1, ta - 1)]
        pltpu.make_async_copy(others, others, sq_sems.at[r, 1]).wait()
        sq_row = sq_ref[r, pl.ds(ti, 1), 0:ch]
        for k in range(1, ta):
            sq_row += sqr_ref[r, k, pl.ds(ti, 1), 0:ch]
        sq_col = jnp.sum(jnp.where(eye[:ch], sq_row, 0.0), axis=1, keepdims=True)
        row_scale = lax.rsqrt(sq_col / (feat * ta) + 1e-5)
        pltpu.make_async_copy(xr_ref.at[r], xr_ref.at[r], c_x.at[r]).wait()
        for i in range(nx - 1):
            total += xr_ref[r, i].astype(F32)
        total = total * row_scale
        acted = jax.nn.silu(total) * pltpu.roll(total, feat - ffd, 1)
        fpad = h_ref.shape[3]
        acted = jnp.where(iota((ch, fpad), 1) < ffd, acted[:, :fpad], 0.0)
        h_ref[r, ti] = acted.astype(BF16)

        for dx in (nx // 2, *[d for d in range(1, nx) if d != nx // 2]):
            pltpu.make_async_remote_copy(
                src_ref=h_ref.at[r, ti],
                dst_ref=h_ref.at[r, ti],
                send_sem=h_send.at[r],
                recv_sem=h_x.at[r, dx],
                device_id=(me, (my_x + dx) % nx * NC + my_c),
                device_id_type=MESH,
            ).start()
        for dx in (0, *[d for d in range(1, nx) if d != nx // 2], nx // 2):
            mine = (my_x + nx - dx) % nx * NC + my_c
            block = h_ref.at[r, mine]
            if dx:
                pltpu.make_async_copy(block, block, h_x.at[r, dx]).wait()
            pltpu.make_async_remote_copy(
                src_ref=block,
                dst_ref=block,
                send_sem=h_send.at[r],
                recv_sem=h_core.at[r],
                device_id=(me, my_x * NC + 1 - my_c),
                device_id_type=MESH,
            ).start()
        landed = h_ref.at[r, pl.ds(0, nx)]
        pltpu.make_async_copy(landed, landed, h_core.at[r]).wait()

        for m in range(2):
            hid = h_ref[r, pl.ds(m * (ta // 2), ta // 2)].reshape(half, fpad)
            down = jnp.dot(hid, d_ref[r], preferred_element_type=F32)
            down = down.reshape(inst // 2, NSTEP, feat)
            part_ref[pl.ds(m * (inst // 2), inst // 2)] = down
            s_ref[r, pl.ds(m * (inst // 2), inst // 2)] = down.astype(BF16)

        def send_y(j, _):
            k = jnp.where(j % 2 == 1, nz // 2 - j // 2, nz // 2 + j // 2)
            k = jnp.where(j == nz, 0, k)
            z = (my_z + k) % nz
            for dy in range(1, ny):
                y = (my_y + dy) % ny
                pltpu.make_async_remote_copy(
                    src_ref=s_ref.at[r, y * nz + z],
                    dst_ref=yr_ref.at[r, k, dy - 1],
                    send_sem=r_send.at[r],
                    recv_sem=r_y.at[r, k],
                    device_id=gdev(y, my_z),
                    device_id_type=MESH,
                ).start()
            return 0

        lax.fori_loop(1, nz + 1, send_y, 0)

        def column_sum(k):
            landed = yr_ref.at[r, k]
            pltpu.make_async_copy(landed, landed, r_y.at[r, k]).wait()
            acc = part_ref[my_y * nz + (my_z + k) % nz]
            for dy in range(ny - 1):
                acc += yr_ref[r, k, dy].astype(F32)
            return acc

        def reduce_y(j, _):
            k = jnp.where(j % 2 == 1, nz // 2 - j // 2, nz // 2 + j // 2)
            zs_ref[r, k] = column_sum(k).astype(BF16)
            pltpu.make_async_remote_copy(
                src_ref=zs_ref.at[r, k],
                dst_ref=zr_ref.at[r, k],
                send_sem=r_send.at[r],
                recv_sem=r_z.at[r],
                device_id=gdev(my_y, (my_z + k) % nz),
                device_id_type=MESH,
            ).start()
            return 0

        lax.fori_loop(1, nz, reduce_y, 0)
        acc = column_sum(0)
        landed = zr_ref.at[r, pl.ds(1, nz - 1)]
        pltpu.make_async_copy(landed, landed, r_z.at[r]).wait()
        for k in range(1, nz):
            acc += zr_ref[r, k].astype(F32)
        node_ref[r + 1, me] = (node_ref[r, me].astype(F32) + acc).astype(BF16)

        @pl.when(r + 1 < ROUNDS)
        def _():
            for c, cut in enumerate(cuts):
                gather_start(r + 1, 2 + c, cut)
            for c, cut in enumerate(cuts):
                gather_forward(r + 1, 2 + c, cut)
            gather_end(r + 1, 2, cuts[0])
            mix(r + 1, 0, cuts[0])
            gather_end(r + 1, 3, cuts[1])

        return 0

    attend(0, cuts[0])
    gather_start(0, 0, cuts[0])
    gather_forward(0, 0, cuts[0])
    attend(1, cuts[1])
    gather_start(0, 1, cuts[1])
    gather_forward(0, 1, cuts[1])
    gather_end(0, 0, cuts[0])
    mix(0, 0, cuts[0])
    gather_end(0, 1, cuts[1])
    lax.fori_loop(0, ROUNDS, one_round, 0)
    out_ref[...] = node_ref[ROUNDS, me]

    sent = kv_send.at[pl.ds(0, gx - 1)]
    pltpu.make_async_copy(sent, sent, kv_send_sem.at[0]).wait()

    @pl.when(has_q)
    def _():
        gone = q_send.at[pl.ds(0, gx - 1)]
        pltpu.make_async_copy(gone, gone, q_send_sem.at[0]).wait()

    n_out = nz - 1 + nz * (ny - 1)
    for s in range(2 * ROUNDS):
        blocks = node_ref.at[0, pl.ds(0, n_out), :, cuts[s % 2]]
        pltpu.make_async_copy(blocks, blocks, n_send.at[s]).wait()

    def drain(r, _):
        blocks = node_ref.at[0, pl.ds(0, n_out)]
        pltpu.make_async_copy(blocks, blocks, r_send.at[r]).wait()
        pltpu.make_async_copy(cs_ref.at[r], cs_ref.at[r], c_send.at[r]).wait()
        pltpu.make_async_copy(xs_ref.at[r], xs_ref.at[r], c_send.at[r]).wait()
        others = sqr_ref.at[r, pl.ds(1, ta - 1)]
        pltpu.make_async_copy(others, others, sq_sems.at[r, 0]).wait()
        hid = h_ref.at[r, pl.ds(0, 2 * nx - 1)]
        pltpu.make_async_copy(hid, hid, h_send.at[r]).wait()
        return 0

    lax.fori_loop(0, ROUNDS, drain, 0)


def per_device(
    query_vecs,
    key_vecs,
    value_vecs,
    slot_map,
    edge_list,
    edge_types,
    type_gain,
    norm_gain,
    gate_proj,
    up_proj,
    down_proj,
):
    gx, ta = lax.axis_size("gx"), lax.axis_size("ta")
    pairs, inst, feat = query_vecs.shape
    ffd = gate_proj.shape[2]
    fpad = pl.cdiv(ffd, 128) * 128
    rows = inst * NSTEP
    nz = NZ if gx >= NZ else gx // 2
    ny = gx // nz
    nx = ta // NC
    ch = rows // ta
    vmem = pl.BlockSpec(memory_space=pltpu.VMEM)
    hbm = pl.BlockSpec(memory_space=pl.ANY)
    dma = pltpu.SemaphoreType.DMA
    R = ROUNDS
    return pl.pallas_call(
        functools.partial(kernel, gx, ta),
        out_shape=jax.ShapeDtypeStruct((NSTEP, feat), BF16),
        in_specs=[hbm, hbm, hbm, vmem, vmem, vmem, vmem, vmem, hbm, hbm, hbm],
        out_specs=vmem,
        scratch_shapes=[
            pltpu.VMEM((3, pairs, inst, feat), BF16),
            pltpu.VMEM((inst, NSTEP, feat), BF16),
            pltpu.VMEM((inst, NSTEP, feat), BF16),
            pltpu.VMEM((inst, pairs, feat), BF16),
            pltpu.VMEM((gx // 2, pairs, feat), BF16),
            pltpu.VMEM((gx // 2 * pairs, feat), F32),
            pltpu.VMEM((R, feat, feat), BF16),
            pltpu.VMEM((R, fpad, feat), BF16),
            pltpu.VMEM((ETYPES, rows, rows), BF16),
            pltpu.VMEM((rows, 128), F32),
            pltpu.VMEM((R + 1, inst, NSTEP, feat), BF16),
            pltpu.VMEM((inst, NSTEP, feat), F32),
            pltpu.VMEM((R, inst, NSTEP, feat), BF16),
            pltpu.VMEM((R, nz, ny - 1, NSTEP, feat), BF16),
            pltpu.VMEM((R, nz, NSTEP, feat), BF16),
            pltpu.VMEM((R, nz, NSTEP, feat), BF16),
            pltpu.VMEM((ta, ch, feat), F32),
            pltpu.VMEM((R, nx, ch, feat), BF16),
            pltpu.VMEM((R, nx, ch, feat), BF16),
            pltpu.VMEM((R, nx - 1, ch, feat), BF16),
            pltpu.VMEM((R, nx - 1, ch, feat), BF16),
            pltpu.VMEM((R, ta, 128), F32),
            pltpu.VMEM((R, ta, ta, 128), F32),
            pltpu.VMEM((R, ta, ch, fpad), BF16),
            pltpu.VMEM((rows, 128), F32),
            dma((3,)),
            dma((3,)),
            dma((2,)),
            dma((2,)),
            dma((1,)),
            dma((1,)),
            dma((2 * R,)),
            dma((2 * R, nz)),
            dma((2 * R,)),
            dma((R,)),
            dma((R, nz)),
            dma((R,)),
            dma((R,)),
            dma((R, nx)),
            dma((R,)),
            dma((R, 2)),
            dma((R,)),
            dma((R, nx)),
            dma((R,)),
        ],
        compiler_params=pltpu.CompilerParams(
            collective_id=0, has_side_effects=True, vmem_limit_bytes=56 << 20
        ),
    )(
        query_vecs,
        key_vecs,
        value_vecs,
        slot_map,
        edge_list.T,
        edge_types[None],
        jnp.swapaxes(type_gain, 0, 1),
        norm_gain,
        jnp.swapaxes(gate_proj, 1, 2),
        jnp.swapaxes(up_proj, 1, 2),
        down_proj,
    )


def solution(mesh):
    placed = (
        P("gx", None, "ta"),
        P("gx", None, "ta"),
        P("gx", None, "ta"),
        P(),
        P(),
        P(),
        P(None, None, "ta"),
        P(None, "ta"),
        P(None, "ta", "gx"),
        P(None, "ta", "gx"),
        P(None, "gx", "ta"),
    )
    return jax.shard_map(
        per_device, mesh=mesh, in_specs=placed, out_specs=P("gx", "ta"), check_vma=False
    )
```

```python
import functools

import jax
import jax.numpy as jnp
from jax import lax
from jax.experimental import pallas as pl
from jax.experimental.pallas import tpu as pltpu
from jax.sharding import PartitionSpec as P

MESH = pl.DeviceIdType.MESH
HEAD = 128
STEPS = 16
NSTEP = 8
ROUNDS = 2
ETYPES = 3
PD = 4
NZ = 16
NC = 2
F32 = jnp.float32
BF16 = jnp.bfloat16
NT = (((1,), (1,)), ((), ()))


def iota(shape, dim):
    return lax.broadcasted_iota(jnp.int32, shape, dim)


def kernel(
    gx,
    ta,
    q_hbm,
    k_hbm,
    v_hbm,
    slot_ref,
    edge_ref,
    type_ref,
    tgain_ref,
    ngain_ref,
    g_hbm,
    u_hbm,
    d_hbm,
    out_ref,
    x_in,
    kv_send,
    kv_recv,
    q_send,
    q_recv,
    q_f32,
    w_ref,
    d_ref,
    adj_ref,
    deg_ref,
    node_ref,
    part_ref,
    s_ref,
    yr_ref,
    zs_ref,
    zr_ref,
    gu_ref,
    cs_ref,
    cr_ref,
    xs_ref,
    xr_ref,
    sq_ref,
    sqr_ref,
    h_ref,
    square_ref,
    in_sem,
    w_sem,
    kv_sems,
    q_sems,
    kv_send_sem,
    q_send_sem,
    n_send,
    n_z,
    n_y,
    r_send,
    r_y,
    r_z,
    c_send,
    c_core,
    c_x,
    sq_sems,
    h_send,
    h_x,
    h_core,
):
    inst = gx
    nz = NZ if gx >= NZ else gx // 2
    ny = gx // nz
    nx = ta // NC
    feat = out_ref.shape[1]
    heads = feat // HEAD
    ffd = feat // 2
    rows = inst * NSTEP
    ch = rows // ta
    half = rows // 2
    c0 = (heads + 1) // 2 * HEAD
    cuts = (pl.ds(0, c0), pl.ds(c0, feat - c0))
    me = lax.axis_index("gx")
    ti = lax.axis_index("ta")
    my_y, my_z = me // nz, me % nz
    my_x, my_c = ti // NC, ti % NC

    def gdev(y, z):
        return (y * nz + z, ti)

    barrier = pltpu.get_barrier_semaphore()

    def greet_gx(k, _):
        pl.semaphore_signal(
            barrier, inc=1, device_id=((me + k) % gx, ti), device_id_type=MESH
        )
        return 0

    lax.fori_loop(1, gx, greet_gx, 0)

    def greet_ta(k, _):
        pl.semaphore_signal(
            barrier, inc=1, device_id=(me, (ti + k) % ta), device_id_type=MESH
        )
        return 0

    lax.fori_loop(1, ta, greet_ta, 0)

    loads = [
        pltpu.make_async_copy(src, x_in.at[i], in_sem.at[i])
        for i, src in enumerate((q_hbm, k_hbm, v_hbm))
    ]
    loads[1].start()
    loads[2].start()
    loads[0].start()
    weights = [
        pltpu.make_async_copy(g_hbm, w_ref.at[:, pl.ds(0, ffd)], w_sem.at[0]),
        pltpu.make_async_copy(u_hbm, w_ref.at[:, pl.ds(ffd, ffd)], w_sem.at[1]),
        pltpu.make_async_copy(d_hbm, d_ref.at[:, pl.ds(0, ffd)], w_sem.at[2]),
    ]

    order = slot_ref[pl.ds(me * PD // STEPS, 1), :].astype(F32)
    r8 = iota((rows, inst), 0)
    pick = jnp.where(iota((rows, inst), 1) == r8 // NSTEP, order, 0.0)
    slot_of = jnp.sum(pick, axis=1, keepdims=True).astype(jnp.int32)
    row = iota((rows, 2 * PD * inst), 0)
    col = iota((rows, 2 * PD * inst), 1)
    perm = jnp.where(col == (row % NSTEP) * inst + slot_of, 1.0, 0.0).astype(BF16)

    loads[1].wait()
    loads[2].wait()
    keyvals = x_in[1:3].reshape(2 * PD * inst, feat)
    kv_send[...] = (
        jnp.dot(perm, keyvals, preferred_element_type=F32)
        .reshape(inst, NSTEP, feat)
        .astype(BF16)
    )
    loads[0].wait()
    queries = x_in[0].reshape(PD * inst, feat)
    q_send[...] = (
        jnp.dot(perm[:, : PD * inst], queries, preferred_element_type=F32)
        .reshape(inst, NSTEP, feat)[:, :PD]
        .astype(BF16)
    )
    pl.semaphore_wait(barrier, gx - 1 + ta - 1)

    def partner(k):
        n = k - 1
        turn, dy = n // ny, (n + 1) % ny
        step = jnp.where(turn % 2 == 1, nz // 2 - (turn + 1) // 2, nz // 2 + turn // 2)
        return (my_y + dy) % ny * nz + (my_z + step) % nz

    def q_slot(g):
        return (g // 4) * 2 + g % 4 - 2

    has_q = me % 4 >= 2

    for c, cut in enumerate(cuts):

        @pl.when(has_q)
        def _(c=c, cut=cut):
            def send_q(k, _):
                dest = partner(k)
                pltpu.make_async_remote_copy(
                    src_ref=q_send.at[dest, :, cut],
                    dst_ref=q_recv.at[q_slot(me), :, cut],
                    send_sem=q_send_sem.at[0],
                    recv_sem=q_sems.at[c],
                    device_id=(dest, ti),
                    device_id_type=MESH,
                ).start()
                return 0

            lax.fori_loop(1, gx, send_q, 0)
            pltpu.make_async_copy(
                q_send.at[me, :, cut], q_recv.at[q_slot(me), :, cut], q_sems.at[c]
            ).start()

        def send_kv(k, _, c=c, cut=cut):
            dest = partner(k)
            pltpu.make_async_remote_copy(
                src_ref=kv_send.at[dest, :, cut],
                dst_ref=kv_recv.at[me, :, cut],
                send_sem=kv_send_sem.at[0],
                recv_sem=kv_sems.at[c],
                device_id=(dest, ti),
                device_id_type=MESH,
            ).start()
            return 0

        lax.fori_loop(1, gx, send_kv, 0)
        pltpu.make_async_copy(
            kv_send.at[me, :, cut], kv_recv.at[me, :, cut], kv_sems.at[c]
        ).start()

    for w in weights:
        w.start()
    src = edge_ref[0:1, :]
    tgt = edge_ref[1:2, :]
    typ = type_ref[...]
    edges = tgt.shape[1]
    inst_of = iota((rows, edges), 0) // NSTEP
    at_target = inst_of == tgt
    at_source = jnp.where(inst_of == src, 1.0, 0.0).astype(BF16)
    same_step = iota((rows, rows), 0) % NSTEP == iota((rows, rows), 1) % NSTEP
    for t in range(ETYPES):
        hit = jnp.where(at_target & (typ == t), 1.0, 0.0).astype(BF16)
        count = lax.dot_general(hit, at_source, NT, preferred_element_type=F32)
        adj_ref[t] = jnp.where(same_step, count, 0.0).astype(BF16)
    degree = jnp.sum(jnp.where(at_target, 1.0, 0.0), axis=1, keepdims=True)
    deg_ref[...] = jnp.broadcast_to(jnp.maximum(degree, 1.0), deg_ref.shape)
    if d_ref.shape[1] > ffd:
        d_ref[:, ffd:, :] = jnp.zeros((ROUNDS, d_ref.shape[1] - ffd, feat), BF16)
    for w in weights:
        w.wait()

    nq = q_f32.shape[0]
    lane = iota((nq, rows), 1)
    key_step = (lane // NSTEP) % 4 * PD + lane % NSTEP
    q_step = iota((nq, rows), 0) % NSTEP + (STEPS - NSTEP)
    allowed = (lane % NSTEP < PD) & (key_step <= q_step)

    def attend(c, cut):
        whole = q_recv.at[:, :, cut]
        pltpu.make_async_copy(whole, whole, q_sems.at[c]).wait()
        for j in range(q_recv.shape[0]):
            q_f32[j * PD : (j + 1) * PD, cut] = q_recv[j, :, cut].astype(F32)
        q_all = q_f32[:, cut].astype(BF16)
        whole = kv_recv.at[:, :, cut]
        pltpu.make_async_copy(whole, whole, kv_sems.at[c]).wait()
        width = cut.size
        kv_all = kv_recv[:, :, cut].astype(F32).reshape(rows, width).astype(BF16)
        pooled = []
        for h in range(width // HEAD):
            own = slice(h * HEAD, (h + 1) * HEAD)
            scores = lax.dot_general(
                q_all[:, own], kv_all[:, own], NT, preferred_element_type=F32
            ) * (1.0 / HEAD**0.5)
            scores = jnp.where(allowed, scores, -1e30)
            expd = jnp.exp(scores - jnp.max(scores, axis=1, keepdims=True))
            probs = expd / jnp.sum(expd, axis=1, keepdims=True)
            probs = pltpu.roll(probs, PD, 1).astype(BF16)
            att = jnp.dot(probs, kv_all[:, own], preferred_element_type=F32)
            pooled.append(jnp.mean(att.reshape(nq // NSTEP, NSTEP, HEAD), axis=0))
        node_ref[0, me, :, cut] = jnp.concatenate(pooled, axis=1).astype(BF16)

    eye = iota((rows, ch), 0) % ch == iota((rows, ch), 1)

    if nz == 16:
        first = (8, 7, 9, 6, 10, 5, 11, 4, 12, 3, 13, 2, 14, 1, 15)
        second = {}
        arrivals = first[::-1]
    else:
        first = arrivals = tuple(range(1, nz))
        second = {}

    def pass_on(r, s, cut, blk):
        for dy in (2, 1, 3):
            if dy < ny:
                pltpu.make_async_remote_copy(
                    src_ref=node_ref.at[r, blk, :, cut],
                    dst_ref=node_ref.at[r, blk, :, cut],
                    send_sem=n_send.at[s],
                    recv_sem=n_y.at[s],
                    device_id=gdev((my_y + dy) % ny, my_z),
                    device_id_type=MESH,
                ).start()

    def send_z(r, s, cut, blk, step, total):
        pltpu.make_async_remote_copy(
            src_ref=node_ref.at[r, blk, :, cut],
            dst_ref=node_ref.at[r, blk, :, cut],
            send_sem=n_send.at[s],
            recv_sem=n_z.at[s, total],
            device_id=gdev(my_y, (my_z + step) % nz),
            device_id_type=MESH,
        ).start()

    def gather_start(r, s, cut):
        for k in first:
            send_z(r, s, cut, me, k, k)
        pass_on(r, s, cut, me)

    def gather_forward(r, s, cut):
        for k in arrivals:
            blk = my_y * nz + (my_z + nz - k) % nz
            landed = node_ref.at[r, blk, :, cut]
            pltpu.make_async_copy(landed, landed, n_z.at[s, k]).wait()
            for more in second.get(k, ()):
                send_z(r, s, cut, blk, more, (k + more) % nz)
            pass_on(r, s, cut, blk)

    def gather_end(r, s, cut):
        arrived = node_ref.at[r, pl.ds(0, (ny - 1) * nz), :, cut]
        pltpu.make_async_copy(arrived, arrived, n_y.at[s]).wait()

    def mix(r, c, cut):
        width = cut.size
        node_f32 = node_ref[r, :, :, cut].astype(F32).reshape(rows, width)
        node_all = node_f32.astype(BF16)
        ngain = ngain_ref[pl.ds(r, 1), cut]
        weight = w_ref[r, :, cut]
        for m in range(2):
            mine = slice(m * half, (m + 1) * half)
            total = jnp.zeros((half, width), F32)
            for t in range(ETYPES):
                total += tgain_ref[t, pl.ds(r, 1), cut] * jnp.dot(
                    adj_ref[t, mine, :], node_all, preferred_element_type=F32
                )
            pre = node_f32[mine] + total / deg_ref[mine, 0:1]
            square = jnp.sum(pre * pre, axis=1, keepdims=True)
            square = jnp.broadcast_to(square, (half, 128))
            scaled = (pre * ngain).astype(BF16)
            sums = lax.dot_general(scaled, weight, NT, preferred_element_type=F32)
            sums = sums.reshape(ta // 2, ch, feat)
            spot = slice(m * (ta // 2), (m + 1) * (ta // 2))
            if c == 0:
                gu_ref[spot] = sums
                square_ref[mine] = square
            else:
                gu_ref[spot] += sums
                square_ref[mine] += square

    def one_round(r, _):
        mix(r, 1, cuts[1])

        def send_sq(k, _):
            pltpu.make_async_remote_copy(
                src_ref=sq_ref.at[r],
                dst_ref=sqr_ref.at[r, k],
                send_sem=sq_sems.at[r, 0],
                recv_sem=sq_sems.at[r, 1],
                device_id=(me, (ti + k) % ta),
                device_id_type=MESH,
            ).start()
            return 0

        for i in range(nx):
            x = (my_x + i + nx // 2) % nx
            cs_ref[r, i] = gu_ref[x * NC + 1 - my_c].astype(BF16)
            pltpu.make_async_remote_copy(
                src_ref=cs_ref.at[r, i],
                dst_ref=cr_ref.at[r, i],
                send_sem=c_send.at[r],
                recv_sem=c_core.at[r, i],
                device_id=(me, my_x * NC + 1 - my_c),
                device_id_type=MESH,
            ).start()
        square = square_ref[:, 0:1]
        by_chunk = jnp.sum(jnp.where(eye, square, 0.0).reshape(ta, ch, ch), axis=1)
        sq_ref[r, :, 0:ch] = by_chunk
        lax.fori_loop(1, ta, send_sq, 0)
        total = jnp.zeros((ch, feat), F32)
        for i in range(nx):
            dx = (i + nx // 2) % nx
            x = (my_x + dx) % nx
            landed = cr_ref.at[r, i]
            pltpu.make_async_copy(landed, landed, c_core.at[r, i]).wait()
            chip_sum = gu_ref[x * NC + my_c] + cr_ref[r, i].astype(F32)
            if dx == 0:
                total = chip_sum
            else:
                xs_ref[r, dx - 1] = chip_sum.astype(BF16)
                pltpu.make_async_remote_copy(
                    src_ref=xs_ref.at[r, dx - 1],
                    dst_ref=xr_ref.at[r, dx - 1],
                    send_sem=c_send.at[r],
                    recv_sem=c_x.at[r],
                    device_id=(me, x * NC + my_c),
                    device_id_type=MESH,
                ).start()
        others = sqr_ref.at[r, pl.ds(1, ta - 1)]
        pltpu.make_async_copy(others, others, sq_sems.at[r, 1]).wait()
        sq_row = sq_ref[r, pl.ds(ti, 1), 0:ch]
        for k in range(1, ta):
            sq_row += sqr_ref[r, k, pl.ds(ti, 1), 0:ch]
        sq_col = jnp.sum(jnp.where(eye[:ch], sq_row, 0.0), axis=1, keepdims=True)
        row_scale = lax.rsqrt(sq_col / (feat * ta) + 1e-5)
        pltpu.make_async_copy(xr_ref.at[r], xr_ref.at[r], c_x.at[r]).wait()
        for i in range(nx - 1):
            total += xr_ref[r, i].astype(F32)
        total = total * row_scale
        acted = jax.nn.silu(total) * pltpu.roll(total, feat - ffd, 1)
        fpad = h_ref.shape[3]
        acted = jnp.where(iota((ch, fpad), 1) < ffd, acted[:, :fpad], 0.0)
        h_ref[r, ti] = acted.astype(BF16)

        for dx in (nx // 2, *[d for d in range(1, nx) if d != nx // 2]):
            pltpu.make_async_remote_copy(
                src_ref=h_ref.at[r, ti],
                dst_ref=h_ref.at[r, ti],
                send_sem=h_send.at[r],
                recv_sem=h_x.at[r, dx],
                device_id=(me, (my_x + dx) % nx * NC + my_c),
                device_id_type=MESH,
            ).start()
        for dx in (0, *[d for d in range(1, nx) if d != nx // 2], nx // 2):
            mine = (my_x + nx - dx) % nx * NC + my_c
            block = h_ref.at[r, mine]
            if dx:
                pltpu.make_async_copy(block, block, h_x.at[r, dx]).wait()
            pltpu.make_async_remote_copy(
                src_ref=block,
                dst_ref=block,
                send_sem=h_send.at[r],
                recv_sem=h_core.at[r],
                device_id=(me, my_x * NC + 1 - my_c),
                device_id_type=MESH,
            ).start()
        landed = h_ref.at[r, pl.ds(0, nx)]
        pltpu.make_async_copy(landed, landed, h_core.at[r]).wait()

        for m in range(2):
            hid = h_ref[r, pl.ds(m * (ta // 2), ta // 2)].reshape(half, fpad)
            down = jnp.dot(hid, d_ref[r], preferred_element_type=F32)
            down = down.reshape(inst // 2, NSTEP, feat)
            part_ref[pl.ds(m * (inst // 2), inst // 2)] = down
            s_ref[r, pl.ds(m * (inst // 2), inst // 2)] = down.astype(BF16)

        def send_y(j, _):
            k = jnp.where(j % 2 == 1, nz // 2 - j // 2, nz // 2 + j // 2)
            k = jnp.where(j == nz, 0, k)
            z = (my_z + k) % nz
            for dy in range(1, ny):
                y = (my_y + dy) % ny
                pltpu.make_async_remote_copy(
                    src_ref=s_ref.at[r, y * nz + z],
                    dst_ref=yr_ref.at[r, k, dy - 1],
                    send_sem=r_send.at[r],
                    recv_sem=r_y.at[r, k],
                    device_id=gdev(y, my_z),
                    device_id_type=MESH,
                ).start()
            return 0

        lax.fori_loop(1, nz + 1, send_y, 0)

        def column_sum(k):
            landed = yr_ref.at[r, k]
            pltpu.make_async_copy(landed, landed, r_y.at[r, k]).wait()
            acc = part_ref[my_y * nz + (my_z + k) % nz]
            for dy in range(ny - 1):
                acc += yr_ref[r, k, dy].astype(F32)
            return acc

        def reduce_y(j, _):
            k = jnp.where(j % 2 == 1, nz // 2 - j // 2, nz // 2 + j // 2)
            zs_ref[r, k] = column_sum(k).astype(BF16)
            pltpu.make_async_remote_copy(
                src_ref=zs_ref.at[r, k],
                dst_ref=zr_ref.at[r, k],
                send_sem=r_send.at[r],
                recv_sem=r_z.at[r],
                device_id=gdev(my_y, (my_z + k) % nz),
                device_id_type=MESH,
            ).start()
            return 0

        lax.fori_loop(1, nz, reduce_y, 0)
        acc = column_sum(0)
        landed = zr_ref.at[r, pl.ds(1, nz - 1)]
        pltpu.make_async_copy(landed, landed, r_z.at[r]).wait()
        for k in range(1, nz):
            acc += zr_ref[r, k].astype(F32)
        node_ref[r + 1, me] = (node_ref[r, me].astype(F32) + acc).astype(BF16)

        @pl.when(r + 1 < ROUNDS)
        def _():
            for c, cut in enumerate(cuts):
                gather_start(r + 1, 2 + c, cut)
            for c, cut in enumerate(cuts):
                gather_forward(r + 1, 2 + c, cut)
            gather_end(r + 1, 2, cuts[0])
            mix(r + 1, 0, cuts[0])
            gather_end(r + 1, 3, cuts[1])

        return 0

    attend(0, cuts[0])
    gather_start(0, 0, cuts[0])
    attend(1, cuts[1])
    gather_start(0, 1, cuts[1])
    gather_forward(0, 0, cuts[0])
    gather_forward(0, 1, cuts[1])
    gather_end(0, 0, cuts[0])
    mix(0, 0, cuts[0])
    gather_end(0, 1, cuts[1])
    lax.fori_loop(0, ROUNDS, one_round, 0)
    out_ref[...] = node_ref[ROUNDS, me]

    sent = kv_send.at[pl.ds(0, gx - 1)]
    pltpu.make_async_copy(sent, sent, kv_send_sem.at[0]).wait()

    @pl.when(has_q)
    def _():
        gone = q_send.at[pl.ds(0, gx - 1)]
        pltpu.make_async_copy(gone, gone, q_send_sem.at[0]).wait()

    n_out = nz - 1 + nz * (ny - 1)
    for s in range(2 * ROUNDS):
        blocks = node_ref.at[0, pl.ds(0, n_out), :, cuts[s % 2]]
        pltpu.make_async_copy(blocks, blocks, n_send.at[s]).wait()

    def drain(r, _):
        blocks = node_ref.at[0, pl.ds(0, n_out)]
        pltpu.make_async_copy(blocks, blocks, r_send.at[r]).wait()
        pltpu.make_async_copy(cs_ref.at[r], cs_ref.at[r], c_send.at[r]).wait()
        pltpu.make_async_copy(xs_ref.at[r], xs_ref.at[r], c_send.at[r]).wait()
        others = sqr_ref.at[r, pl.ds(1, ta - 1)]
        pltpu.make_async_copy(others, others, sq_sems.at[r, 0]).wait()
        hid = h_ref.at[r, pl.ds(0, 2 * nx - 1)]
        pltpu.make_async_copy(hid, hid, h_send.at[r]).wait()
        return 0

    lax.fori_loop(0, ROUNDS, drain, 0)


def per_device(
    query_vecs,
    key_vecs,
    value_vecs,
    slot_map,
    edge_list,
    edge_types,
    type_gain,
    norm_gain,
    gate_proj,
    up_proj,
    down_proj,
):
    gx, ta = lax.axis_size("gx"), lax.axis_size("ta")
    pairs, inst, feat = query_vecs.shape
    ffd = gate_proj.shape[2]
    fpad = pl.cdiv(ffd, 128) * 128
    rows = inst * NSTEP
    nz = NZ if gx >= NZ else gx // 2
    ny = gx // nz
    nx = ta // NC
    ch = rows // ta
    vmem = pl.BlockSpec(memory_space=pltpu.VMEM)
    hbm = pl.BlockSpec(memory_space=pl.ANY)
    dma = pltpu.SemaphoreType.DMA
    R = ROUNDS
    return pl.pallas_call(
        functools.partial(kernel, gx, ta),
        out_shape=jax.ShapeDtypeStruct((NSTEP, feat), BF16),
        in_specs=[hbm, hbm, hbm, vmem, vmem, vmem, vmem, vmem, hbm, hbm, hbm],
        out_specs=vmem,
        scratch_shapes=[
            pltpu.VMEM((3, pairs, inst, feat), BF16),
            pltpu.VMEM((inst, NSTEP, feat), BF16),
            pltpu.VMEM((inst, NSTEP, feat), BF16),
            pltpu.VMEM((inst, pairs, feat), BF16),
            pltpu.VMEM((gx // 2, pairs, feat), BF16),
            pltpu.VMEM((gx // 2 * pairs, feat), F32),
            pltpu.VMEM((R, feat, feat), BF16),
            pltpu.VMEM((R, fpad, feat), BF16),
            pltpu.VMEM((ETYPES, rows, rows), BF16),
            pltpu.VMEM((rows, 128), F32),
            pltpu.VMEM((R + 1, inst, NSTEP, feat), BF16),
            pltpu.VMEM((inst, NSTEP, feat), F32),
            pltpu.VMEM((R, inst, NSTEP, feat), BF16),
            pltpu.VMEM((R, nz, ny - 1, NSTEP, feat), BF16),
            pltpu.VMEM((R, nz, NSTEP, feat), BF16),
            pltpu.VMEM((R, nz, NSTEP, feat), BF16),
            pltpu.VMEM((ta, ch, feat), F32),
            pltpu.VMEM((R, nx, ch, feat), BF16),
            pltpu.VMEM((R, nx, ch, feat), BF16),
            pltpu.VMEM((R, nx - 1, ch, feat), BF16),
            pltpu.VMEM((R, nx - 1, ch, feat), BF16),
            pltpu.VMEM((R, ta, 128), F32),
            pltpu.VMEM((R, ta, ta, 128), F32),
            pltpu.VMEM((R, ta, ch, fpad), BF16),
            pltpu.VMEM((rows, 128), F32),
            dma((3,)),
            dma((3,)),
            dma((2,)),
            dma((2,)),
            dma((1,)),
            dma((1,)),
            dma((2 * R,)),
            dma((2 * R, nz)),
            dma((2 * R,)),
            dma((R,)),
            dma((R, nz)),
            dma((R,)),
            dma((R,)),
            dma((R, nx)),
            dma((R,)),
            dma((R, 2)),
            dma((R,)),
            dma((R, nx)),
            dma((R,)),
        ],
        compiler_params=pltpu.CompilerParams(
            collective_id=0, has_side_effects=True, vmem_limit_bytes=56 << 20
        ),
    )(
        query_vecs,
        key_vecs,
        value_vecs,
        slot_map,
        edge_list.T,
        edge_types[None],
        jnp.swapaxes(type_gain, 0, 1),
        norm_gain,
        jnp.swapaxes(gate_proj, 1, 2),
        jnp.swapaxes(up_proj, 1, 2),
        down_proj,
    )


def solution(mesh):
    placed = (
        P("gx", None, "ta"),
        P("gx", None, "ta"),
        P("gx", None, "ta"),
        P(),
        P(),
        P(),
        P(None, None, "ta"),
        P(None, "ta"),
        P(None, "ta", "gx"),
        P(None, "ta", "gx"),
        P(None, "gx", "ta"),
    )
    return jax.shard_map(
        per_device, mesh=mesh, in_specs=placed, out_specs=P("gx", "ta"), check_vma=False
    )
```

```python
import functools

import jax
import jax.numpy as jnp
from jax import lax
from jax.experimental import pallas as pl
from jax.experimental.pallas import tpu as pltpu
from jax.sharding import PartitionSpec as P

MESH = pl.DeviceIdType.MESH
HEAD = 128
STEPS = 16
NSTEP = 8
ROUNDS = 2
ETYPES = 3
PD = 4
NZ = 16
NC = 2
F32 = jnp.float32
BF16 = jnp.bfloat16
NT = (((1,), (1,)), ((), ()))


def iota(shape, dim):
    return lax.broadcasted_iota(jnp.int32, shape, dim)


def kernel(
    gx,
    ta,
    q_hbm,
    k_hbm,
    v_hbm,
    slot_ref,
    edge_ref,
    type_ref,
    tgain_ref,
    ngain_ref,
    g_hbm,
    u_hbm,
    d_hbm,
    out_ref,
    x_in,
    kv_send,
    kv_recv,
    q_send,
    q_recv,
    q_f32,
    w_ref,
    d_ref,
    adj_ref,
    deg_ref,
    node_ref,
    part_ref,
    s_ref,
    yr_ref,
    zs_ref,
    zr_ref,
    gu_ref,
    cs_ref,
    cr_ref,
    xs_ref,
    xr_ref,
    sq_ref,
    sqr_ref,
    h_ref,
    square_ref,
    in_sem,
    w_sem,
    kv_sems,
    q_sems,
    kv_send_sem,
    q_send_sem,
    n_send,
    n_z,
    n_y,
    r_send,
    r_y,
    r_z,
    c_send,
    c_core,
    c_x,
    sq_sems,
    h_send,
    h_x,
    h_core,
):
    inst = gx
    nz = NZ if gx >= NZ else gx // 2
    ny = gx // nz
    nx = ta // NC
    feat = out_ref.shape[1]
    heads = feat // HEAD
    ffd = feat // 2
    rows = inst * NSTEP
    ch = rows // ta
    half = rows // 2
    c0 = (heads + 1) // 2 * HEAD
    cuts = (pl.ds(0, c0), pl.ds(c0, feat - c0))
    me = lax.axis_index("gx")
    ti = lax.axis_index("ta")
    my_y, my_z = me // nz, me % nz
    my_x, my_c = ti // NC, ti % NC

    def gdev(y, z):
        return (y * nz + z, ti)

    barrier = pltpu.get_barrier_semaphore()

    def greet_gx(k, _):
        pl.semaphore_signal(
            barrier, inc=1, device_id=((me + k) % gx, ti), device_id_type=MESH
        )
        return 0

    lax.fori_loop(1, gx, greet_gx, 0)

    def greet_ta(k, _):
        pl.semaphore_signal(
            barrier, inc=1, device_id=(me, (ti + k) % ta), device_id_type=MESH
        )
        return 0

    lax.fori_loop(1, ta, greet_ta, 0)

    loads = [
        pltpu.make_async_copy(src, x_in.at[i], in_sem.at[i])
        for i, src in enumerate((q_hbm, k_hbm, v_hbm))
    ]
    loads[1].start()
    loads[2].start()
    loads[0].start()
    weights = [
        pltpu.make_async_copy(g_hbm, w_ref.at[:, pl.ds(0, ffd)], w_sem.at[0]),
        pltpu.make_async_copy(u_hbm, w_ref.at[:, pl.ds(ffd, ffd)], w_sem.at[1]),
        pltpu.make_async_copy(d_hbm, d_ref.at[:, pl.ds(0, ffd)], w_sem.at[2]),
    ]

    order = slot_ref[pl.ds(me * PD // STEPS, 1), :].astype(F32)
    r8 = iota((rows, inst), 0)
    pick = jnp.where(iota((rows, inst), 1) == r8 // NSTEP, order, 0.0)
    slot_of = jnp.sum(pick, axis=1, keepdims=True).astype(jnp.int32)
    row = iota((rows, 2 * PD * inst), 0)
    col = iota((rows, 2 * PD * inst), 1)
    perm = jnp.where(col == (row % NSTEP) * inst + slot_of, 1.0, 0.0).astype(BF16)

    loads[1].wait()
    loads[2].wait()
    keyvals = x_in[1:3].reshape(2 * PD * inst, feat)
    kv_send[...] = (
        jnp.dot(perm, keyvals, preferred_element_type=F32)
        .reshape(inst, NSTEP, feat)
        .astype(BF16)
    )
    loads[0].wait()
    queries = x_in[0].reshape(PD * inst, feat)
    q_send[...] = (
        jnp.dot(perm[:, : PD * inst], queries, preferred_element_type=F32)
        .reshape(inst, NSTEP, feat)[:, :PD]
        .astype(BF16)
    )
    pl.semaphore_wait(barrier, gx - 1 + ta - 1)

    def partner(k):
        n = k - 1
        turn, dy = n // ny, (n + 1) % ny
        step = jnp.where(turn % 2 == 1, nz // 2 - (turn + 1) // 2, nz // 2 + turn // 2)
        return (my_y + dy) % ny * nz + (my_z + step) % nz

    def q_slot(g):
        return (g // 4) * 2 + g % 4 - 2

    has_q = me % 4 >= 2

    for c, cut in enumerate(cuts):

        @pl.when(has_q)
        def _(c=c, cut=cut):
            def send_q(k, _):
                dest = partner(k)
                pltpu.make_async_remote_copy(
                    src_ref=q_send.at[dest, :, cut],
                    dst_ref=q_recv.at[q_slot(me), :, cut],
                    send_sem=q_send_sem.at[0],
                    recv_sem=q_sems.at[c],
                    device_id=(dest, ti),
                    device_id_type=MESH,
                ).start()
                return 0

            lax.fori_loop(1, gx, send_q, 0)
            pltpu.make_async_copy(
                q_send.at[me, :, cut], q_recv.at[q_slot(me), :, cut], q_sems.at[c]
            ).start()

        def send_kv(k, _, c=c, cut=cut):
            dest = partner(k)
            pltpu.make_async_remote_copy(
                src_ref=kv_send.at[dest, :, cut],
                dst_ref=kv_recv.at[me, :, cut],
                send_sem=kv_send_sem.at[0],
                recv_sem=kv_sems.at[c],
                device_id=(dest, ti),
                device_id_type=MESH,
            ).start()
            return 0

        lax.fori_loop(1, gx, send_kv, 0)
        pltpu.make_async_copy(
            kv_send.at[me, :, cut], kv_recv.at[me, :, cut], kv_sems.at[c]
        ).start()

    for w in weights:
        w.start()
    src = edge_ref[0:1, :]
    tgt = edge_ref[1:2, :]
    typ = type_ref[...]
    edges = tgt.shape[1]
    inst_of = iota((rows, edges), 0) // NSTEP
    at_target = inst_of == tgt
    at_source = jnp.where(inst_of == src, 1.0, 0.0).astype(BF16)
    same_step = iota((rows, rows), 0) % NSTEP == iota((rows, rows), 1) % NSTEP
    for t in range(ETYPES):
        hit = jnp.where(at_target & (typ == t), 1.0, 0.0).astype(BF16)
        count = lax.dot_general(hit, at_source, NT, preferred_element_type=F32)
        adj_ref[t] = jnp.where(same_step, count, 0.0).astype(BF16)
    degree = jnp.sum(jnp.where(at_target, 1.0, 0.0), axis=1, keepdims=True)
    deg_ref[...] = jnp.broadcast_to(jnp.maximum(degree, 1.0), deg_ref.shape)
    if d_ref.shape[1] > ffd:
        d_ref[:, ffd:, :] = jnp.zeros((ROUNDS, d_ref.shape[1] - ffd, feat), BF16)
    for w in weights:
        w.wait()

    nq = q_f32.shape[0]
    lane = iota((nq, rows), 1)
    key_step = (lane // NSTEP) % 4 * PD + lane % NSTEP
    q_step = iota((nq, rows), 0) % NSTEP + (STEPS - NSTEP)
    allowed = (lane % NSTEP < PD) & (key_step <= q_step)

    def attend(c, cut):
        whole = q_recv.at[:, :, cut]
        pltpu.make_async_copy(whole, whole, q_sems.at[c]).wait()
        for j in range(q_recv.shape[0]):
            q_f32[j * PD : (j + 1) * PD, cut] = q_recv[j, :, cut].astype(F32)
        q_all = q_f32[:, cut].astype(BF16)
        whole = kv_recv.at[:, :, cut]
        pltpu.make_async_copy(whole, whole, kv_sems.at[c]).wait()
        width = cut.size
        kv_all = kv_recv[:, :, cut].astype(F32).reshape(rows, width).astype(BF16)
        pooled = []
        for h in range(width // HEAD):
            own = slice(h * HEAD, (h + 1) * HEAD)
            scores = lax.dot_general(
                q_all[:, own], kv_all[:, own], NT, preferred_element_type=F32
            ) * (1.0 / HEAD**0.5)
            scores = jnp.where(allowed, scores, -1e30)
            expd = jnp.exp(scores - jnp.max(scores, axis=1, keepdims=True))
            probs = expd / jnp.sum(expd, axis=1, keepdims=True)
            probs = pltpu.roll(probs, PD, 1).astype(BF16)
            att = jnp.dot(probs, kv_all[:, own], preferred_element_type=F32)
            pooled.append(jnp.mean(att.reshape(nq // NSTEP, NSTEP, HEAD), axis=0))
        node_ref[0, me, :, cut] = jnp.concatenate(pooled, axis=1).astype(BF16)

    eye = iota((rows, ch), 0) % ch == iota((rows, ch), 1)

    if nz == 16:
        first = (8, 7, 9, 6, 10, 5, 11, 4, 12, 3, 13, 2, 14, 1, 15)
        second = {}
        arrivals = first[::-1]
    else:
        first = arrivals = tuple(range(1, nz))
        second = {}

    def pass_on(r, s, cut, blk):
        for dy in (2, 1, 3):
            if dy < ny:
                pltpu.make_async_remote_copy(
                    src_ref=node_ref.at[r, blk, :, cut],
                    dst_ref=node_ref.at[r, blk, :, cut],
                    send_sem=n_send.at[s],
                    recv_sem=n_y.at[s],
                    device_id=gdev((my_y + dy) % ny, my_z),
                    device_id_type=MESH,
                ).start()

    def send_z(r, s, cut, blk, step, total):
        pltpu.make_async_remote_copy(
            src_ref=node_ref.at[r, blk, :, cut],
            dst_ref=node_ref.at[r, blk, :, cut],
            send_sem=n_send.at[s],
            recv_sem=n_z.at[s, total],
            device_id=gdev(my_y, (my_z + step) % nz),
            device_id_type=MESH,
        ).start()

    def gather_start(r, s, cut):
        for k in first:
            send_z(r, s, cut, me, k, k)
        pass_on(r, s, cut, me)

    def gather_forward(r, s, cut):
        for k in arrivals:
            blk = my_y * nz + (my_z + nz - k) % nz
            landed = node_ref.at[r, blk, :, cut]
            pltpu.make_async_copy(landed, landed, n_z.at[s, k]).wait()
            for more in second.get(k, ()):
                send_z(r, s, cut, blk, more, (k + more) % nz)
            pass_on(r, s, cut, blk)

    def gather_end(r, s, cut):
        arrived = node_ref.at[r, pl.ds(0, (ny - 1) * nz), :, cut]
        pltpu.make_async_copy(arrived, arrived, n_y.at[s]).wait()

    def mix(r, c, cut):
        width = cut.size
        node_f32 = node_ref[r, :, :, cut].astype(F32).reshape(rows, width)
        node_all = node_f32.astype(BF16)
        ngain = ngain_ref[pl.ds(r, 1), cut]
        weight = w_ref[r, :, cut]
        for m in range(2):
            mine = slice(m * half, (m + 1) * half)
            total = jnp.zeros((half, width), F32)
            for t in range(ETYPES):
                total += tgain_ref[t, pl.ds(r, 1), cut] * jnp.dot(
                    adj_ref[t, mine, :], node_all, preferred_element_type=F32
                )
            pre = node_f32[mine] + total / deg_ref[mine, 0:1]
            square = jnp.sum(pre * pre, axis=1, keepdims=True)
            square = jnp.broadcast_to(square, (half, 128))
            scaled = (pre * ngain).astype(BF16)
            sums = lax.dot_general(scaled, weight, NT, preferred_element_type=F32)
            sums = sums.reshape(ta // 2, ch, feat)
            spot = slice(m * (ta // 2), (m + 1) * (ta // 2))
            if c == 0:
                gu_ref[spot] = sums
                square_ref[mine] = square
            else:
                gu_ref[spot] += sums
                square_ref[mine] += square

    def one_round(r, _):
        mix(r, 1, cuts[1])

        def send_sq(k, _):
            pltpu.make_async_remote_copy(
                src_ref=sq_ref.at[r],
                dst_ref=sqr_ref.at[r, k],
                send_sem=sq_sems.at[r, 0],
                recv_sem=sq_sems.at[r, 1],
                device_id=(me, (ti + k) % ta),
                device_id_type=MESH,
            ).start()
            return 0

        for i in range(nx):
            x = (my_x + i + nx // 2) % nx
            cs_ref[r, i] = gu_ref[x * NC + 1 - my_c].astype(BF16)
            pltpu.make_async_remote_copy(
                src_ref=cs_ref.at[r, i],
                dst_ref=cr_ref.at[r, i],
                send_sem=c_send.at[r],
                recv_sem=c_core.at[r, i],
                device_id=(me, my_x * NC + 1 - my_c),
                device_id_type=MESH,
            ).start()
        square = square_ref[:, 0:1]
        by_chunk = jnp.sum(jnp.where(eye, square, 0.0).reshape(ta, ch, ch), axis=1)
        sq_ref[r, :, 0:ch] = by_chunk
        lax.fori_loop(1, ta, send_sq, 0)
        total = jnp.zeros((ch, feat), F32)
        for i in range(nx):
            dx = (i + nx // 2) % nx
            x = (my_x + dx) % nx
            landed = cr_ref.at[r, i]
            pltpu.make_async_copy(landed, landed, c_core.at[r, i]).wait()
            chip_sum = gu_ref[x * NC + my_c] + cr_ref[r, i].astype(F32)
            if dx == 0:
                total = chip_sum
            else:
                xs_ref[r, dx - 1] = chip_sum.astype(BF16)
                pltpu.make_async_remote_copy(
                    src_ref=xs_ref.at[r, dx - 1],
                    dst_ref=xr_ref.at[r, dx - 1],
                    send_sem=c_send.at[r],
                    recv_sem=c_x.at[r],
                    device_id=(me, x * NC + my_c),
                    device_id_type=MESH,
                ).start()
        others = sqr_ref.at[r, pl.ds(1, ta - 1)]
        pltpu.make_async_copy(others, others, sq_sems.at[r, 1]).wait()
        sq_row = sq_ref[r, pl.ds(ti, 1), 0:ch]
        for k in range(1, ta):
            sq_row += sqr_ref[r, k, pl.ds(ti, 1), 0:ch]
        sq_col = jnp.sum(jnp.where(eye[:ch], sq_row, 0.0), axis=1, keepdims=True)
        row_scale = lax.rsqrt(sq_col / (feat * ta) + 1e-5)
        pltpu.make_async_copy(xr_ref.at[r], xr_ref.at[r], c_x.at[r]).wait()
        for i in range(nx - 1):
            total += xr_ref[r, i].astype(F32)
        total = total * row_scale
        acted = jax.nn.silu(total) * pltpu.roll(total, feat - ffd, 1)
        fpad = h_ref.shape[3]
        acted = jnp.where(iota((ch, fpad), 1) < ffd, acted[:, :fpad], 0.0)
        h_ref[r, ti] = acted.astype(BF16)

        for dx in (nx // 2, *[d for d in range(1, nx) if d != nx // 2]):
            pltpu.make_async_remote_copy(
                src_ref=h_ref.at[r, ti],
                dst_ref=h_ref.at[r, ti],
                send_sem=h_send.at[r],
                recv_sem=h_x.at[r, dx],
                device_id=(me, (my_x + dx) % nx * NC + my_c),
                device_id_type=MESH,
            ).start()
        for dx in (0, *[d for d in range(1, nx) if d != nx // 2], nx // 2):
            mine = (my_x + nx - dx) % nx * NC + my_c
            block = h_ref.at[r, mine]
            if dx:
                pltpu.make_async_copy(block, block, h_x.at[r, dx]).wait()
            pltpu.make_async_remote_copy(
                src_ref=block,
                dst_ref=block,
                send_sem=h_send.at[r],
                recv_sem=h_core.at[r],
                device_id=(me, my_x * NC + 1 - my_c),
                device_id_type=MESH,
            ).start()
        landed = h_ref.at[r, pl.ds(0, nx)]
        pltpu.make_async_copy(landed, landed, h_core.at[r]).wait()

        for m in range(2):
            hid = h_ref[r, pl.ds(m * (ta // 2), ta // 2)].reshape(half, fpad)
            down = jnp.dot(hid, d_ref[r], preferred_element_type=F32)
            down = down.reshape(inst // 2, NSTEP, feat)
            part_ref[pl.ds(m * (inst // 2), inst // 2)] = down
            s_ref[r, pl.ds(m * (inst // 2), inst // 2)] = down.astype(BF16)

        for c, cut in enumerate(cuts):

            def send_y(j, _, c=c, cut=cut):
                k = jnp.where(j % 2 == 1, nz // 2 - j // 2, nz // 2 + j // 2)
                k = jnp.where(j == nz, 0, k)
                z = (my_z + k) % nz
                for dy in range(1, ny):
                    y = (my_y + dy) % ny
                    pltpu.make_async_remote_copy(
                        src_ref=s_ref.at[r, y * nz + z, :, cut],
                        dst_ref=yr_ref.at[r, k, dy - 1, :, cut],
                        send_sem=r_send.at[r],
                        recv_sem=r_y.at[2 * r + c, k],
                        device_id=gdev(y, my_z),
                        device_id_type=MESH,
                    ).start()
                return 0

            lax.fori_loop(1, nz + 1, send_y, 0)

        def column_sum(k, c, cut):
            landed = yr_ref.at[r, k, :, :, cut]
            pltpu.make_async_copy(landed, landed, r_y.at[2 * r + c, k]).wait()
            acc = part_ref[my_y * nz + (my_z + k) % nz, :, cut]
            for dy in range(ny - 1):
                acc += yr_ref[r, k, dy, :, cut].astype(F32)
            return acc

        for c, cut in enumerate(cuts):

            def reduce_y(j, _, c=c, cut=cut):
                k = jnp.where(j % 2 == 1, nz // 2 - j // 2, nz // 2 + j // 2)
                zs_ref[r, k, :, cut] = column_sum(k, c, cut).astype(BF16)
                pltpu.make_async_remote_copy(
                    src_ref=zs_ref.at[r, k, :, cut],
                    dst_ref=zr_ref.at[r, k, :, cut],
                    send_sem=r_send.at[r],
                    recv_sem=r_z.at[2 * r + c],
                    device_id=gdev(my_y, (my_z + k) % nz),
                    device_id_type=MESH,
                ).start()
                return 0

            lax.fori_loop(1, nz, reduce_y, 0)
        for c, cut in enumerate(cuts):
            acc = column_sum(0, c, cut)
            landed = zr_ref.at[r, pl.ds(1, nz - 1), :, cut]
            pltpu.make_async_copy(landed, landed, r_z.at[2 * r + c]).wait()
            for k in range(1, nz):
                acc += zr_ref[r, k, :, cut].astype(F32)
            acc += node_ref[r, me, :, cut].astype(F32)
            node_ref[r + 1, me, :, cut] = acc.astype(BF16)

            @pl.when(r + 1 < ROUNDS)
            def _(c=c, cut=cut):
                gather_start(r + 1, 2 + c, cut)

        @pl.when(r + 1 < ROUNDS)
        def _():
            for c, cut in enumerate(cuts):
                gather_forward(r + 1, 2 + c, cut)
            gather_end(r + 1, 2, cuts[0])
            mix(r + 1, 0, cuts[0])
            gather_end(r + 1, 3, cuts[1])

        return 0

    attend(0, cuts[0])
    gather_start(0, 0, cuts[0])
    attend(1, cuts[1])
    gather_start(0, 1, cuts[1])
    gather_forward(0, 0, cuts[0])
    gather_forward(0, 1, cuts[1])
    gather_end(0, 0, cuts[0])
    mix(0, 0, cuts[0])
    gather_end(0, 1, cuts[1])
    lax.fori_loop(0, ROUNDS, one_round, 0)
    out_ref[...] = node_ref[ROUNDS, me]

    sent = kv_send.at[pl.ds(0, gx - 1)]
    pltpu.make_async_copy(sent, sent, kv_send_sem.at[0]).wait()

    @pl.when(has_q)
    def _():
        gone = q_send.at[pl.ds(0, gx - 1)]
        pltpu.make_async_copy(gone, gone, q_send_sem.at[0]).wait()

    n_out = nz - 1 + nz * (ny - 1)
    for s in range(2 * ROUNDS):
        blocks = node_ref.at[0, pl.ds(0, n_out), :, cuts[s % 2]]
        pltpu.make_async_copy(blocks, blocks, n_send.at[s]).wait()

    def drain(r, _):
        blocks = node_ref.at[0, pl.ds(0, n_out)]
        pltpu.make_async_copy(blocks, blocks, r_send.at[r]).wait()
        pltpu.make_async_copy(cs_ref.at[r], cs_ref.at[r], c_send.at[r]).wait()
        pltpu.make_async_copy(xs_ref.at[r], xs_ref.at[r], c_send.at[r]).wait()
        others = sqr_ref.at[r, pl.ds(1, ta - 1)]
        pltpu.make_async_copy(others, others, sq_sems.at[r, 0]).wait()
        hid = h_ref.at[r, pl.ds(0, 2 * nx - 1)]
        pltpu.make_async_copy(hid, hid, h_send.at[r]).wait()
        return 0

    lax.fori_loop(0, ROUNDS, drain, 0)


def per_device(
    query_vecs,
    key_vecs,
    value_vecs,
    slot_map,
    edge_list,
    edge_types,
    type_gain,
    norm_gain,
    gate_proj,
    up_proj,
    down_proj,
):
    gx, ta = lax.axis_size("gx"), lax.axis_size("ta")
    pairs, inst, feat = query_vecs.shape
    ffd = gate_proj.shape[2]
    fpad = pl.cdiv(ffd, 128) * 128
    rows = inst * NSTEP
    nz = NZ if gx >= NZ else gx // 2
    ny = gx // nz
    nx = ta // NC
    ch = rows // ta
    vmem = pl.BlockSpec(memory_space=pltpu.VMEM)
    hbm = pl.BlockSpec(memory_space=pl.ANY)
    dma = pltpu.SemaphoreType.DMA
    R = ROUNDS
    return pl.pallas_call(
        functools.partial(kernel, gx, ta),
        out_shape=jax.ShapeDtypeStruct((NSTEP, feat), BF16),
        in_specs=[hbm, hbm, hbm, vmem, vmem, vmem, vmem, vmem, hbm, hbm, hbm],
        out_specs=vmem,
        scratch_shapes=[
            pltpu.VMEM((3, pairs, inst, feat), BF16),
            pltpu.VMEM((inst, NSTEP, feat), BF16),
            pltpu.VMEM((inst, NSTEP, feat), BF16),
            pltpu.VMEM((inst, pairs, feat), BF16),
            pltpu.VMEM((gx // 2, pairs, feat), BF16),
            pltpu.VMEM((gx // 2 * pairs, feat), F32),
            pltpu.VMEM((R, feat, feat), BF16),
            pltpu.VMEM((R, fpad, feat), BF16),
            pltpu.VMEM((ETYPES, rows, rows), BF16),
            pltpu.VMEM((rows, 128), F32),
            pltpu.VMEM((R + 1, inst, NSTEP, feat), BF16),
            pltpu.VMEM((inst, NSTEP, feat), F32),
            pltpu.VMEM((R, inst, NSTEP, feat), BF16),
            pltpu.VMEM((R, nz, ny - 1, NSTEP, feat), BF16),
            pltpu.VMEM((R, nz, NSTEP, feat), BF16),
            pltpu.VMEM((R, nz, NSTEP, feat), BF16),
            pltpu.VMEM((ta, ch, feat), F32),
            pltpu.VMEM((R, nx, ch, feat), BF16),
            pltpu.VMEM((R, nx, ch, feat), BF16),
            pltpu.VMEM((R, nx - 1, ch, feat), BF16),
            pltpu.VMEM((R, nx - 1, ch, feat), BF16),
            pltpu.VMEM((R, ta, 128), F32),
            pltpu.VMEM((R, ta, ta, 128), F32),
            pltpu.VMEM((R, ta, ch, fpad), BF16),
            pltpu.VMEM((rows, 128), F32),
            dma((3,)),
            dma((3,)),
            dma((2,)),
            dma((2,)),
            dma((1,)),
            dma((1,)),
            dma((2 * R,)),
            dma((2 * R, nz)),
            dma((2 * R,)),
            dma((R,)),
            dma((2 * R, nz)),
            dma((2 * R,)),
            dma((R,)),
            dma((R, nx)),
            dma((R,)),
            dma((R, 2)),
            dma((R,)),
            dma((R, nx)),
            dma((R,)),
        ],
        compiler_params=pltpu.CompilerParams(
            collective_id=0, has_side_effects=True, vmem_limit_bytes=56 << 20
        ),
    )(
        query_vecs,
        key_vecs,
        value_vecs,
        slot_map,
        edge_list.T,
        edge_types[None],
        jnp.swapaxes(type_gain, 0, 1),
        norm_gain,
        jnp.swapaxes(gate_proj, 1, 2),
        jnp.swapaxes(up_proj, 1, 2),
        down_proj,
    )


def solution(mesh):
    placed = (
        P("gx", None, "ta"),
        P("gx", None, "ta"),
        P("gx", None, "ta"),
        P(),
        P(),
        P(),
        P(None, None, "ta"),
        P(None, "ta"),
        P(None, "ta", "gx"),
        P(None, "ta", "gx"),
        P(None, "gx", "ta"),
    )
    return jax.shard_map(
        per_device, mesh=mesh, in_specs=placed, out_specs=P("gx", "ta"), check_vma=False
    )
```
